32 devices in a mesh: groups: 2 (over x), expert: 16 (over z, y, core).
Axes of the slice: x: 2, y: 2, z: 4, core: 2. Of those that a mesh axis runs over, the one named last changes fastest.
Arguments:
- out_grad: bfloat16 [4096, 2560], P(('groups', 'expert')), parts along dimension 0, may hold values from -6 to 6
- saved_hidden: bfloat16 [4096, 6, 768], P(('groups', 'expert')), parts along dimension 0, may hold values from -0.21875 to 0.21875
- expert_ids: int32 [4096, 6], P(('groups', 'expert')), parts along dimension 0, may hold values from 0 to 15, as said below
- gate_weights: bfloat16 [4096, 6], P(('groups', 'expert')), parts along dimension 0, may hold values from 0.049804688 to 0.5
- trained: int32 [32], P(('groups', 'expert')), parts along dimension 0, may hold values 0 or 1
- down_weight: bfloat16 [16, 768, 2560], P('expert'), may hold values from -0.125 to 0.125
Outputs:
- hidden_grad: bfloat16 [4096, 6, 768], P(('groups', 'expert')), parts along dimension 0
- gate_grad: bfloat16 [4096, 6], P(('groups', 'expert')), parts along dimension 0
- weight_grad: bfloat16 [32, 768, 2560], P(('groups', 'expert')), parts along dimension 0
The draws below stay inside these ranges and needn't reach their ends.
There are 2 independent parts, one for each index of `groups`. The reference program is written for one: setup_inputs(seed, part) draws one part's arguments, and reference() takes and returns one part's arrays. A program takes and returns all parts, laid end to end along the dimension named above; an argument that names none is the same for every part. Nothing has to cross between parts.
Inputs may be any that keep to these rules, and one draw needn't show every extreme that they name: `expert_ids`: each row names 6 different experts. The rows of one device name any one expert at most 72 times, and some expert is named exactly 72 times by the rows of every device.
All inputs are finite; a program needn't handle non-finite values. No bound on the sum of `trained` on one device may be relied on, other than what follows from the above.
Results may differ from the reference program's by a relative error of at most 0.0085.
Values may be sent and summed in bfloat16 or wider, within the bound.
No kernel may reach another device: no remote copies, remote signals or barrier semaphores. Data moves between devices by JAX's collectives and lax.ppermute only.
A program may use at most 128 MiB of HBM per device.

```python
import jax
import jax.numpy as jnp
from jax import lax

D = 2560
H = 768
TOPK = 6
TOK_DEV = 128
ROUTED_EXPERTS = 16
TOKENS = 2048
MOST = 72


def draw_expert_ids(key, part):
    blocks = TOKENS // TOK_DEV
    slot_count = TOK_DEV * TOPK
    expert_order = jax.random.permutation(jax.random.fold_in(key, 11), ROUTED_EXPERTS).astype(jnp.int32)
    hot_expert = expert_order[0]
    others = expert_order[1:]
    base_count = (slot_count - MOST) // (ROUTED_EXPERTS - 1)
    surplus_count = slot_count - MOST - base_count * (ROUTED_EXPERTS - 1)
    shift_reach = min(base_count, MOST - base_count - 1)
    pair_count = (ROUTED_EXPERTS - 1) // 2

    def single_block(block_index):
        block_key = jax.random.fold_in(key, block_index)
        permuted_rows = others[jax.random.permutation(jax.random.fold_in(block_key, 1), ROUTED_EXPERTS - 1)]
        shifts = jax.random.randint(jax.random.fold_in(block_key, 2), (pair_count,), 0, shift_reach + 1).astype(jnp.int32)
        expert_counts = jnp.zeros((ROUTED_EXPERTS,), jnp.int32) + base_count
        expert_counts = expert_counts.at[hot_expert].set(MOST)
        expert_counts = expert_counts.at[permuted_rows[:pair_count]].add(shifts)
        expert_counts = expert_counts.at[permuted_rows[pair_count:2 * pair_count]].add(-shifts)
        surplus_rows = (jnp.arange(ROUTED_EXPERTS - 1) < surplus_count).astype(jnp.int32)
        expert_counts = expert_counts.at[permuted_rows].add(surplus_rows)
        run_ends = jnp.cumsum(expert_counts)
        sequence = jnp.sum((run_ends[None, :] <= jnp.arange(slot_count, dtype=jnp.int32)[:, None]).astype(jnp.int32), axis=1)
        slot_grid = sequence.reshape(TOPK, TOK_DEV).T
        row_order = jax.random.permutation(jax.random.fold_in(block_key, 3), TOK_DEV)
        return slot_grid[row_order]
    drawn = lax.map(single_block, jnp.arange(blocks, dtype=jnp.int32))
    return drawn.reshape(TOKENS, TOPK).astype(jnp.int32)


def plant(entries, rng, low, top_value):
    longest = entries.shape.index(max(entries.shape))
    spots = []
    for shift in (0, 1):
        where = [jax.random.randint(jax.random.fold_in(rng, axis), (), 0, length) for axis, length in enumerate(entries.shape)]
        where[longest] = (where[longest] + shift) % entries.shape[longest]
        spots.append(tuple(where))
    return entries.at[spots[0]].set(low).at[spots[1]].set(top_value)


def steps_of(key, extent, cuts, low, largest):
    loudness, own = 1.0, jax.random.fold_in(key, 6)
    for position, blocks in cuts:
        heights = jnp.exp(jax.random.uniform(jax.random.fold_in(own, position), (blocks,), jnp.float32, low / len(cuts), largest / len(cuts)))
        loudness = loudness * jnp.repeat(heights, extent[position] // blocks).reshape([-1 if axis == position else 1 for axis in range(len(extent))])
    return loudness


def bell_draw(stream_key, extent, deviation, limit, shards=(), kind=jnp.bfloat16):
    result = deviation * jax.random.normal(stream_key, extent, jnp.float32)
    if shards:
        result = result * steps_of(stream_key, extent, shards, -0.22, 0.18)
    return jnp.clip(result, -limit, limit).astype(kind)


def setup_inputs(seed: int = 0, part: int = 0) -> dict:
    key_of = jax.random.split(jax.random.key(seed), 7)
    part_splits = jax.random.split(jax.random.fold_in(key_of[6], part), 7)
    out_grad = bell_draw(part_splits[0], (TOKENS, D), 1.0, 6.0, ((0, 16),))
    saved_hidden = bell_draw(part_splits[1], (TOKENS, TOPK, H), H ** -0.5, 0.21875, ((0, 16),))
    expert_ids = draw_expert_ids(jax.random.fold_in(jax.random.fold_in(key_of[6], part), 71), part)
    gate_weights = jnp.clip(0.049804688 + 0.4501953 * jax.random.uniform(part_splits[3], (TOKENS, TOPK), jnp.float32) ** steps_of(part_splits[3], (TOKENS, TOPK), ((0, 16),), -0.2, 0.2), 0.049804688, 0.5).astype(jnp.bfloat16)
    trained = plant((jax.random.randint(part_splits[4], (ROUTED_EXPERTS,), 0, 2) < 1).astype(jnp.int32), jax.random.fold_in(part_splits[4], 1), 0, 1)
    down_weight = bell_draw(key_of[5], (ROUTED_EXPERTS, H, D), D ** -0.5, 0.125, ((0, 16),))
    return dict(out_grad=out_grad, saved_hidden=saved_hidden, expert_ids=expert_ids, gate_weights=gate_weights, trained=trained, down_weight=down_weight)


def reference(out_grad, saved_hidden, expert_ids, gate_weights, trained, down_weight):
    slot_count = TOKENS * TOPK
    capacity = (TOKENS // TOK_DEV) * MOST
    flat_ids = expert_ids.reshape(slot_count).astype(jnp.int32)
    onehot = (flat_ids[:, None] == jnp.arange(ROUTED_EXPERTS, dtype=jnp.int32)[None, :]).astype(jnp.int32)
    slot_rank = jnp.sum(jnp.cumsum(onehot, axis=0) * onehot, axis=1) - 1
    table = jnp.full((ROUTED_EXPERTS, capacity), slot_count, jnp.int32)
    table = table.at[flat_ids, slot_rank].set(jnp.arange(slot_count, dtype=jnp.int32))
    grad_table = jnp.concatenate([out_grad, jnp.zeros((1, D), out_grad.dtype)], axis=0)
    hidden_table = jnp.concatenate([saved_hidden.reshape(slot_count, H), jnp.zeros((1, H), saved_hidden.dtype)], axis=0)
    gate_table = jnp.concatenate([gate_weights.reshape(slot_count), jnp.zeros((1,), gate_weights.dtype)], axis=0)

    def per_expert(expert_index):
        slot_selections = table[expert_index]
        token_selections = jnp.where(slot_selections < slot_count, slot_selections // TOPK, TOKENS).astype(jnp.int32)
        grad_rows = grad_table[token_selections]
        hidden_rows = hidden_table[slot_selections]
        gate_col = gate_table[slot_selections].astype(jnp.float32)[:, None]
        weight = down_weight[expert_index]
        upstream = lax.dot_general(grad_rows, weight, (((1,), (1,)), ((), ())), preferred_element_type=jnp.float32).astype(jnp.bfloat16)
        upstream = lax.optimization_barrier(upstream)
        upstream_wide = upstream.astype(jnp.float32)
        hidden_part = (gate_col * upstream_wide).astype(jnp.bfloat16)
        gate_part = jnp.sum(hidden_rows.astype(jnp.float32) * upstream_wide, axis=1).astype(jnp.bfloat16)
        scaled = (gate_col * grad_rows.astype(jnp.float32)).astype(jnp.bfloat16)
        weight_sum = lax.dot_general(hidden_rows, scaled, (((0,), (0,)), ((), ())), preferred_element_type=jnp.float32)
        weight_part = (weight_sum * trained[expert_index].astype(jnp.float32)).astype(jnp.bfloat16)
        return hidden_part, gate_part, weight_part

    hidden_all, gate_all, weight_grad = lax.map(per_expert, jnp.arange(ROUTED_EXPERTS, dtype=jnp.int32))
    flat_table = table.reshape(ROUTED_EXPERTS * capacity)
    hidden_grad = jnp.zeros((slot_count + 1, H), jnp.bfloat16).at[flat_table].set(hidden_all.reshape(ROUTED_EXPERTS * capacity, H))
    gate_grad = jnp.zeros((slot_count + 1,), jnp.bfloat16).at[flat_table].set(gate_all.reshape(ROUTED_EXPERTS * capacity))
    hidden_grad = hidden_grad[:slot_count].reshape(TOKENS, TOPK, H)
    gate_grad = gate_grad[:slot_count].reshape(TOKENS, TOPK)
    return hidden_grad, gate_grad, weight_grad
```

```python
import functools

import jax
import jax.numpy as jnp
from jax import lax
from jax.experimental import pallas as pl
from jax.experimental.pallas import tpu as pltpu
from jax.sharding import PartitionSpec as P

F32, BF16, I32 = jnp.float32, jnp.bfloat16, jnp.int32
VMEM_LIMIT = 48 * 1024 * 1024


def whole(memory_space=pltpu.VMEM):
    return pl.BlockSpec(memory_space=memory_space)


def earlier(tokens):
    row = lax.broadcasted_iota(I32, (tokens, tokens), 0)
    column = lax.broadcasted_iota(I32, (tokens, tokens), 1)
    return (row < column).astype(F32).astype(BF16)


def pack_kernel(experts, capacity, ids_ref, gates_ref, hidden_ref, out_ref, place_ref, table, select):
    top_count, tokens = ids_ref.shape
    expert = lax.broadcasted_iota(I32, (experts, tokens), 0)
    named = jnp.zeros((experts, tokens), F32)
    for k in range(top_count):
        named = named + (ids_ref[k : k + 1, :] == expert).astype(F32)
    rank = jnp.dot(named.astype(BF16), earlier(tokens), preferred_element_type=F32).astype(I32)
    target = expert * capacity + rank
    for k in range(top_count):
        place_ref[k : k + 1, :] = jnp.sum(
            jnp.where(ids_ref[k : k + 1, :] == expert, target, 0), axis=0, keepdims=True
        )
        table[k * tokens : (k + 1) * tokens, :] = hidden_ref[:, k, :]
    rows = out_ref.shape[0]
    step = 128
    for first in range(0, rows, step):
        row = lax.broadcasted_iota(I32, (step, tokens), 0) + first
        for k in range(top_count):
            select[:, k * tokens : (k + 1) * tokens] = jnp.where(
                place_ref[k : k + 1, :] == row, gates_ref[k : k + 1, :].astype(F32), 0.0
            ).astype(BF16)
        out_ref[first : first + step, :] = jnp.dot(
            select[...], table[...], preferred_element_type=F32
        ).astype(BF16)


def pack(ids_t, gates_t, saved_hidden, experts, capacity):
    tokens, top_count, hidden_units = saved_hidden.shape
    return pl.pallas_call(
        functools.partial(pack_kernel, experts, capacity),
        out_shape=(
            jax.ShapeDtypeStruct((experts * capacity, hidden_units), BF16),
            jax.ShapeDtypeStruct((top_count, tokens), I32),
        ),
        in_specs=[whole()] * 3,
        out_specs=(whole(), whole()),
        scratch_shapes=[
            pltpu.VMEM((top_count * tokens, hidden_units), BF16),
            pltpu.VMEM((128, top_count * tokens), BF16),
        ],
        compiler_params=pltpu.CompilerParams(vmem_limit_bytes=VMEM_LIMIT),
        name="pack",
    )(ids_t, gates_t, saved_hidden)


def source_rank(ids, expert, tokens):
    named = jnp.max((ids == expert).astype(F32), axis=0, keepdims=True)
    rank = jnp.dot(named.astype(BF16), earlier(tokens), preferred_element_type=F32)
    return jnp.where(named > 0.5, rank.astype(I32), -1)


def upstream_kernel(capacity, expert_ref, ids_ref, grad_ref, weight_ref, out_ref):
    tokens = grad_ref.shape[0]
    dense = lax.dot_general(
        grad_ref[...], weight_ref[...], (((1,), (1,)), ((), ())), preferred_element_type=F32
    ).astype(BF16)
    rank = source_rank(ids_ref[0], expert_ref[0], tokens)
    choose = (rank == lax.broadcasted_iota(I32, (capacity, tokens), 0)).astype(F32).astype(BF16)
    out_ref[0] = jnp.dot(choose, dense, preferred_element_type=F32).astype(BF16)


def upstream(expert, ids_all, grads, weight, capacity):
    sources, top_count, tokens = ids_all.shape
    hidden_units, width = weight.shape
    return pl.pallas_call(
        functools.partial(upstream_kernel, capacity),
        out_shape=jax.ShapeDtypeStruct((sources, capacity, hidden_units), BF16),
        grid_spec=pltpu.PrefetchScalarGridSpec(
            num_scalar_prefetch=1,
            grid=(sources,),
            in_specs=[
                pl.BlockSpec((1, top_count, tokens), lambda j, e: (j, 0, 0)),
                pl.BlockSpec((tokens, width), lambda j, e: (j, 0)),
                pl.BlockSpec((hidden_units, width), lambda j, e: (0, 0)),
            ],
            out_specs=pl.BlockSpec((1, capacity, hidden_units), lambda j, e: (j, 0, 0)),
        ),
        compiler_params=pltpu.CompilerParams(vmem_limit_bytes=VMEM_LIMIT),
        name="upstream",
    )(expert, ids_all, grads, weight)


def weight_kernel(scalar_ref, ids_ref, hidden_ref, grad_ref, out_ref, dense):
    sources, top_count, tokens = ids_ref.shape
    capacity = hidden_ref.shape[1]

    @pl.when(pl.program_id(0) == 0)
    def _():
        for j in range(sources):
            rank = source_rank(ids_ref[j], scalar_ref[0], tokens)
            choose = (rank == lax.broadcasted_iota(I32, (capacity, tokens), 0)).astype(F32).astype(BF16)
            dense[:, j * tokens : (j + 1) * tokens] = lax.dot_general(
                hidden_ref[j], choose, (((0,), (0,)), ((), ())), preferred_element_type=F32
            ).astype(BF16)

    total = jnp.dot(dense[...], grad_ref[...], preferred_element_type=F32)
    out_ref[...] = (total * scalar_ref[1].astype(F32)).astype(BF16)


def weight_sum(scalars, ids_all, recv_hidden, grads):
    sources, capacity, hidden_units = recv_hidden.shape
    _, top_count, tokens = ids_all.shape
    rows, width = grads.shape
    step = 256
    return pl.pallas_call(
        weight_kernel,
        out_shape=jax.ShapeDtypeStruct((hidden_units, width), BF16),
        grid_spec=pltpu.PrefetchScalarGridSpec(
            num_scalar_prefetch=1,
            grid=(width // step,),
            in_specs=[
                pl.BlockSpec((sources, top_count, tokens), lambda n, e: (0, 0, 0)),
                pl.BlockSpec((sources, capacity, hidden_units), lambda n, e: (0, 0, 0)),
                pl.BlockSpec((rows, step), lambda n, e: (0, n)),
            ],
            out_specs=pl.BlockSpec((hidden_units, step), lambda n, e: (0, n)),
            scratch_shapes=[pltpu.VMEM((hidden_units, rows), BF16)],
        ),
        compiler_params=pltpu.CompilerParams(vmem_limit_bytes=VMEM_LIMIT),
        name="weight_sum",
    )(scalars, ids_all, recv_hidden, grads)


def unpack_kernel(place_ref, gates_ref, hidden_ref, back_ref, grad_ref, gate_ref, select):
    tokens, top_count = place_ref.shape
    rows = back_ref.shape[0]
    for k in range(top_count):
        lane = lax.broadcasted_iota(I32, (tokens, rows), 1)
        select[...] = (place_ref[:, k : k + 1] == lane).astype(F32).astype(BF16)
        up = jnp.dot(select[...], back_ref[...], preferred_element_type=F32)
        grad_ref[:, k, :] = (gates_ref[:, k : k + 1].astype(F32) * up).astype(BF16)
        gate_ref[:, k : k + 1] = jnp.sum(
            hidden_ref[:, k, :].astype(F32) * up, axis=1, keepdims=True
        ).astype(BF16)


def unpack(place, gates, saved_hidden, back):
    tokens, top_count, hidden_units = saved_hidden.shape
    return pl.pallas_call(
        unpack_kernel,
        out_shape=(
            jax.ShapeDtypeStruct((tokens, top_count, hidden_units), BF16),
            jax.ShapeDtypeStruct((tokens, top_count), BF16),
        ),
        in_specs=[whole()] * 4,
        out_specs=(whole(), whole()),
        scratch_shapes=[pltpu.VMEM((tokens, back.shape[0]), BF16)],
        compiler_params=pltpu.CompilerParams(vmem_limit_bytes=VMEM_LIMIT),
        name="unpack",
    )(place, gates, saved_hidden, back)


def local(out_grad, saved_hidden, expert_ids, gate_weights, trained, down_weight):
    experts = lax.axis_size("expert")
    tokens, top_count, hidden_units = saved_hidden.shape
    capacity = min(tokens, 3 * tokens * top_count // (2 * experts))
    ids_t = expert_ids.T
    me = lax.axis_index("expert").astype(I32)
    ids_all = lax.all_gather(ids_t, "expert", axis=0)
    grads = lax.all_gather(out_grad, "expert", axis=0, tiled=True)
    packed, place_t = pack(ids_t, gate_weights.T, saved_hidden, experts, capacity)
    recv_hidden = lax.all_to_all(
        packed.reshape(experts, capacity, hidden_units), "expert", 0, 0, tiled=True
    )
    up = upstream(me[None], ids_all, grads, down_weight[0], capacity)
    back = lax.all_to_all(up, "expert", 0, 0, tiled=True)
    weight_grad = weight_sum(jnp.stack([me, trained[0]]), ids_all, recv_hidden, grads)
    hidden_grad, gate_grad = unpack(
        place_t.T, gate_weights, saved_hidden, back.reshape(experts * capacity, hidden_units)
    )
    return hidden_grad, gate_grad, weight_grad[None]


def solution(mesh):
    placed = (
        P(("groups", "expert"), None),
        P(("groups", "expert"), None, None),
        P(("groups", "expert"), None),
        P(("groups", "expert"), None),
        P(("groups", "expert")),
        P("expert", None, None),
    )
    return jax.shard_map(
        local,
        mesh=mesh,
        in_specs=placed,
        out_specs=(
            P(("groups", "expert"), None, None),
            P(("groups", "expert"), None),
            P(("groups", "expert"), None, None),
        ),
        check_vma=False,
    )
```

```python
import functools

import jax
import jax.numpy as jnp
from jax import lax
from jax.experimental import pallas as pl
from jax.experimental.pallas import tpu as pltpu
from jax.sharding import PartitionSpec as P

F32, BF16, I32 = jnp.float32, jnp.bfloat16, jnp.int32
VMEM_LIMIT = 48 * 1024 * 1024


def whole(memory_space=pltpu.VMEM):
    return pl.BlockSpec(memory_space=memory_space)


def earlier(tokens):
    row = lax.broadcasted_iota(I32, (tokens, tokens), 0)
    column = lax.broadcasted_iota(I32, (tokens, tokens), 1)
    return (row < column).astype(F32).astype(BF16)


def pack_kernel(experts, capacity, ids_ref, gates_ref, hidden_ref, out_ref, place_ref, table, select):
    top_count, tokens = ids_ref.shape
    expert = lax.broadcasted_iota(I32, (experts, tokens), 0)
    named = jnp.zeros((experts, tokens), F32)
    for k in range(top_count):
        named = named + (ids_ref[k : k + 1, :] == expert).astype(F32)
    rank = jnp.dot(named.astype(BF16), earlier(tokens), preferred_element_type=F32).astype(I32)
    target = expert * capacity + rank
    for k in range(top_count):
        place_ref[k : k + 1, :] = jnp.sum(
            jnp.where(ids_ref[k : k + 1, :] == expert, target, 0), axis=0, keepdims=True
        )
        table[k * tokens : (k + 1) * tokens, :] = hidden_ref[k]
    rows = out_ref.shape[0]
    step = 128
    for first in range(0, rows, step):
        row = lax.broadcasted_iota(I32, (step, tokens), 0) + first
        for k in range(top_count):
            select[:, k * tokens : (k + 1) * tokens] = jnp.where(
                place_ref[k : k + 1, :] == row, gates_ref[k : k + 1, :].astype(F32), 0.0
            ).astype(BF16)
        out_ref[first : first + step, :] = jnp.dot(
            select[...], table[...], preferred_element_type=F32
        ).astype(BF16)


def pack(ids_t, gates_t, hidden_t, experts, capacity):
    top_count, tokens, hidden_units = hidden_t.shape
    return pl.pallas_call(
        functools.partial(pack_kernel, experts, capacity),
        out_shape=(
            jax.ShapeDtypeStruct((experts * capacity, hidden_units), BF16),
            jax.ShapeDtypeStruct((top_count, tokens), I32),
        ),
        in_specs=[whole()] * 3,
        out_specs=(whole(), whole()),
        scratch_shapes=[
            pltpu.VMEM((top_count * tokens, hidden_units), BF16),
            pltpu.VMEM((128, top_count * tokens), BF16),
        ],
        compiler_params=pltpu.CompilerParams(vmem_limit_bytes=VMEM_LIMIT),
        name="pack",
    )(ids_t, gates_t, hidden_t)


def source_rank(ids, expert, tokens):
    named = jnp.max((ids == expert).astype(F32), axis=0, keepdims=True)
    rank = jnp.dot(named.astype(BF16), earlier(tokens), preferred_element_type=F32)
    return jnp.where(named > 0.5, rank.astype(I32), -1)


def upstream_kernel(capacity, expert_ref, ids_ref, grad_ref, weight_ref, out_ref):
    tokens = grad_ref.shape[0]
    dense = lax.dot_general(
        grad_ref[...], weight_ref[...], (((1,), (1,)), ((), ())), preferred_element_type=F32
    ).astype(BF16)
    rank = source_rank(ids_ref[0], expert_ref[0], tokens)
    choose = (rank == lax.broadcasted_iota(I32, (capacity, tokens), 0)).astype(F32).astype(BF16)
    out_ref[0] = jnp.dot(choose, dense, preferred_element_type=F32).astype(BF16)


def upstream(expert, ids_all, grads, weight, capacity):
    sources, top_count, tokens = ids_all.shape
    hidden_units, width = weight.shape
    return pl.pallas_call(
        functools.partial(upstream_kernel, capacity),
        out_shape=jax.ShapeDtypeStruct((sources, capacity, hidden_units), BF16),
        grid_spec=pltpu.PrefetchScalarGridSpec(
            num_scalar_prefetch=1,
            grid=(sources,),
            in_specs=[
                pl.BlockSpec((1, top_count, tokens), lambda j, e: (j, 0, 0)),
                pl.BlockSpec((tokens, width), lambda j, e: (j, 0)),
                pl.BlockSpec((hidden_units, width), lambda j, e: (0, 0)),
            ],
            out_specs=pl.BlockSpec((1, capacity, hidden_units), lambda j, e: (j, 0, 0)),
        ),
        compiler_params=pltpu.CompilerParams(vmem_limit_bytes=VMEM_LIMIT),
        name="upstream",
    )(expert, ids_all, grads, weight)


def weight_kernel(scalar_ref, ids_ref, hidden_ref, grad_ref, out_ref, dense):
    sources, top_count, tokens = ids_ref.shape
    capacity = hidden_ref.shape[1]

    @pl.when(pl.program_id(0) == 0)
    def _():
        for j in range(sources):
            rank = source_rank(ids_ref[j], scalar_ref[0], tokens)
            choose = (rank == lax.broadcasted_iota(I32, (capacity, tokens), 0)).astype(F32).astype(BF16)
            dense[:, j * tokens : (j + 1) * tokens] = lax.dot_general(
                hidden_ref[j], choose, (((0,), (0,)), ((), ())), preferred_element_type=F32
            ).astype(BF16)

    total = jnp.dot(dense[...], grad_ref[...], preferred_element_type=F32)
    out_ref[...] = (total * scalar_ref[1].astype(F32)).astype(BF16)


def weight_sum(scalars, ids_all, recv_hidden, grads):
    sources, capacity, hidden_units = recv_hidden.shape
    _, top_count, tokens = ids_all.shape
    rows, width = grads.shape
    step = 256
    return pl.pallas_call(
        weight_kernel,
        out_shape=jax.ShapeDtypeStruct((hidden_units, width), BF16),
        grid_spec=pltpu.PrefetchScalarGridSpec(
            num_scalar_prefetch=1,
            grid=(width // step,),
            in_specs=[
                pl.BlockSpec((sources, top_count, tokens), lambda n, e: (0, 0, 0)),
                pl.BlockSpec((sources, capacity, hidden_units), lambda n, e: (0, 0, 0)),
                pl.BlockSpec((rows, step), lambda n, e: (0, n)),
            ],
            out_specs=pl.BlockSpec((hidden_units, step), lambda n, e: (0, n)),
            scratch_shapes=[pltpu.VMEM((hidden_units, rows), BF16)],
        ),
        compiler_params=pltpu.CompilerParams(vmem_limit_bytes=VMEM_LIMIT),
        name="weight_sum",
    )(scalars, ids_all, recv_hidden, grads)


RING_STEPS = 4


def ring_device(position, core):
    z, y = (position, 0) if position < 4 else (7 - position, 1)
    return (z * 2 + y) * 2 + core


def ring_shift(step):
    return [
        (ring_device(p, core), ring_device((p + step) % 8, core)) for p in range(8) for core in range(2)
    ]


def ring_gather(block, ids_t, packed):
    half = block.shape[0] // 2
    ids_all = lax.all_to_all(jnp.broadcast_to(ids_t[None], (16, *ids_t.shape)), "expert", 0, 0, tiled=True)
    ahead = behind = block
    pieces = [block]
    for step in range(RING_STEPS - 1):
        ahead = lax.ppermute(ahead, "expert", ring_shift(1))
        behind = lax.ppermute(behind, "expert", ring_shift(-1))
        if step == 1:
            ahead, behind, ids_all, packed = lax.optimization_barrier((ahead, behind, ids_all, packed))
        pieces += [ahead, behind]
    pieces += [
        lax.ppermute(ahead[:half], "expert", ring_shift(1)),
        lax.ppermute(behind[half:], "expert", ring_shift(-1)),
    ]
    pieces[7], pieces[8], packed = lax.optimization_barrier((pieces[7], pieces[8], packed))
    swap = [(i, i ^ 1) for i in range(16)]
    return ids_all, packed, pieces + [lax.ppermute(piece, "expert", swap) for piece in pieces]


OFFSETS = (0, -1, 1, -2, 2, -3, 3, 4)


def slot_source(me, slot):
    chip, core = me // 2, me % 2
    z, y = chip // 2, chip % 2
    position = jnp.where(y == 0, z, 7 - z)
    other = (position + OFFSETS[slot // 2] + 8) % 8
    oz = jnp.where(other < 4, other, 7 - other)
    oy = jnp.where(other < 4, 0, 1)
    return (oz * 2 + oy) * 2 + (core + slot % 2) % 2


def fetches(piece_refs, grads, sems, tokens):
    per_core = len(piece_refs) // 2
    copies = []
    for slot in range(16):
        refs = piece_refs[(slot % 2) * per_core :]
        i = slot // 2
        parts = [refs[i]] if i < 7 else [refs[7], refs[8]]
        at = slot * tokens
        mine = []
        for n, part in enumerate(parts):
            mine.append(
                pltpu.make_async_copy(part, grads.at[pl.ds(at, part.shape[0])], sems.at[slot, n])
            )
            at += part.shape[0]
        copies.append(mine)
    return copies


def ring_upstream_kernel(capacity, me_ref, ids_ref, weight_ref, *rest):
    pieces, (out_ref, grads, sems) = rest[:18], rest[18:]
    tokens = ids_ref.shape[2]
    copies = fetches(pieces, grads, sems, tokens)
    for mine in copies:
        for copy in mine:
            copy.start()
    group = 4
    for first in range(0, 16, group):
        for mine in copies[first : first + group]:
            for copy in mine:
                copy.wait()
        dense = lax.dot_general(
            grads[first * tokens : (first + group) * tokens, :],
            weight_ref[...],
            (((1,), (1,)), ((), ())),
            preferred_element_type=F32,
        ).astype(BF16)
        for slot in range(first, first + group):
            source = slot_source(me_ref[0], slot)
            rank = source_rank(ids_ref[source], me_ref[0], tokens)
            row = lax.broadcasted_iota(I32, (capacity, tokens), 0)
            choose = (rank == row).astype(F32).astype(BF16)
            at = (slot - first) * tokens
            out_ref[source] = jnp.dot(
                choose, dense[at : at + tokens, :], preferred_element_type=F32
            ).astype(BF16)


def ring_upstream(me, ids_all, pieces, weight, capacity):
    sources, top_count, tokens = ids_all.shape
    hidden_units, width = weight.shape
    return pl.pallas_call(
        functools.partial(ring_upstream_kernel, capacity),
        out_shape=jax.ShapeDtypeStruct((sources, capacity, hidden_units), BF16),
        in_specs=[whole(pltpu.SMEM), whole(), whole()] + [whole(pl.ANY)] * 18,
        out_specs=whole(),
        scratch_shapes=[
            pltpu.VMEM((sources * tokens, width), BF16),
            pltpu.SemaphoreType.DMA((16, 2)),
        ],
        compiler_params=pltpu.CompilerParams(vmem_limit_bytes=VMEM_LIMIT),
        cost_estimate=pl.CostEstimate(
            flops=2 * sources * tokens * hidden_units * width,
            bytes_accessed=2 * (sources * tokens + hidden_units) * width,
            transcendentals=0,
        ),
        name="upstream",
    )(me, ids_all, weight, *pieces)


def ring_weight_kernel(scalar_ref, ids_ref, hidden_ref, *rest):
    pieces, (out_ref, grads, sems, dense) = rest[:18], rest[18:]
    tokens = ids_ref.shape[2]
    capacity = hidden_ref.shape[1]
    copies = fetches(pieces, grads, sems, tokens)
    for mine in copies:
        for copy in mine:
            copy.start()
    for slot in range(16):
        source = slot_source(scalar_ref[0], slot)
        rank = source_rank(ids_ref[source], scalar_ref[0], tokens)
        row = lax.broadcasted_iota(I32, (capacity, tokens), 0)
        choose = (rank == row).astype(F32).astype(BF16)
        dense[:, slot * tokens : (slot + 1) * tokens] = lax.dot_general(
            hidden_ref[source], choose, (((0,), (0,)), ((), ())), preferred_element_type=F32
        ).astype(BF16)
    for mine in copies:
        for copy in mine:
            copy.wait()
    width = grads.shape[1]
    step = 256

    @pl.loop(0, width // step)
    def _(n):
        at = pl.ds(pl.multiple_of(n * step, step), step)
        total = jnp.dot(dense[...], grads[:, at], preferred_element_type=F32)
        out_ref[:, at] = (total * scalar_ref[1].astype(F32)).astype(BF16)


def ring_weight_sum(scalars, ids_all, recv_hidden, pieces):
    sources, capacity, hidden_units = recv_hidden.shape
    _, top_count, tokens = ids_all.shape
    width = pieces[0].shape[1]
    return pl.pallas_call(
        ring_weight_kernel,
        out_shape=jax.ShapeDtypeStruct((hidden_units, width), BF16),
        in_specs=[whole(pltpu.SMEM), whole(), whole()] + [whole(pl.ANY)] * 18,
        out_specs=whole(),
        scratch_shapes=[
            pltpu.VMEM((sources * tokens, width), BF16),
            pltpu.SemaphoreType.DMA((16, 2)),
            pltpu.VMEM((hidden_units, sources * tokens), BF16),
        ],
        compiler_params=pltpu.CompilerParams(vmem_limit_bytes=VMEM_LIMIT),
        cost_estimate=pl.CostEstimate(
            flops=2 * sources * tokens * hidden_units * width,
            bytes_accessed=2 * (sources * tokens + hidden_units) * width,
            transcendentals=0,
        ),
        name="weight_sum",
    )(scalars, ids_all, recv_hidden, *pieces)


def unpack_kernel(place_ref, gates_ref, hidden_ref, back_ref, grad_ref, gate_ref, select, sums):
    tokens, top_count = place_ref.shape
    rows = back_ref.shape[0]
    lane = lax.broadcasted_iota(I32, (tokens, rows), 1)
    for k in range(top_count):
        select[k * tokens : (k + 1) * tokens, :] = (
            (place_ref[:, k : k + 1] == lane).astype(F32).astype(BF16)
        )
    sums[...] = jnp.zeros_like(sums)
    up = jnp.dot(select[...], back_ref[...], preferred_element_type=F32)
    for k in range(top_count):
        mine = up[k * tokens : (k + 1) * tokens, :]
        grad_ref[k] = (gates_ref[:, k : k + 1].astype(F32) * mine).astype(BF16)
        sums[:, k : k + 1] = jnp.sum(hidden_ref[k].astype(F32) * mine, axis=1, keepdims=True)
    gate_ref[...] = sums[...].T[:top_count, :].astype(BF16)


def unpack(place, gates, hidden_t, back):
    top_count, tokens, hidden_units = hidden_t.shape
    return pl.pallas_call(
        unpack_kernel,
        out_shape=(
            jax.ShapeDtypeStruct((top_count, tokens, hidden_units), BF16),
            jax.ShapeDtypeStruct((top_count, tokens), BF16),
        ),
        in_specs=[whole()] * 4,
        out_specs=(whole(), whole()),
        scratch_shapes=[
            pltpu.VMEM((top_count * tokens, back.shape[0]), BF16),
            pltpu.VMEM((tokens, 128), F32),
        ],
        compiler_params=pltpu.CompilerParams(vmem_limit_bytes=VMEM_LIMIT),
        name="unpack",
    )(place, gates, hidden_t, back)


def local(out_grad, saved_hidden, expert_ids, gate_weights, trained, down_weight):
    experts = lax.axis_size("expert")
    tokens, top_count, hidden_units = saved_hidden.shape
    capacity = min(tokens, 3 * tokens * top_count // (2 * experts))
    ids_t = expert_ids.T
    hidden_t = saved_hidden.transpose(1, 0, 2)
    me = lax.axis_index("expert").astype(I32)
    scalars = jnp.stack([me, trained[0]])
    packed, place_t = pack(ids_t, gate_weights.T, hidden_t, experts, capacity)
    if experts == 16:
        ids_all, packed, grads = ring_gather(out_grad, ids_t, packed)
        make_upstream, make_weight = ring_upstream, ring_weight_sum
    else:
        ids_all = lax.all_gather(ids_t, "expert", axis=0)
        grads = lax.all_gather(out_grad, "expert", axis=0, tiled=True)
        make_upstream, make_weight = upstream, weight_sum
    recv_hidden = lax.all_to_all(
        packed.reshape(experts, capacity, hidden_units), "expert", 0, 0, tiled=True
    )
    up = make_upstream(me[None], ids_all, grads, down_weight[0], capacity)
    back = lax.all_to_all(up, "expert", 0, 0, tiled=True)
    weight_grad = make_weight(scalars, ids_all, recv_hidden, grads)
    hidden_grad, gate_grad = unpack(
        place_t.T, gate_weights, hidden_t, back.reshape(experts * capacity, hidden_units)
    )
    return hidden_grad.transpose(1, 0, 2), gate_grad.T, weight_grad[None]


def solution(mesh):
    placed = (
        P(("groups", "expert"), None),
        P(("groups", "expert"), None, None),
        P(("groups", "expert"), None),
        P(("groups", "expert"), None),
        P(("groups", "expert")),
        P("expert", None, None),
    )
    return jax.shard_map(
        local,
        mesh=mesh,
        in_specs=placed,
        out_specs=(
            P(("groups", "expert"), None, None),
            P(("groups", "expert"), None),
            P(("groups", "expert"), None, None),
        ),
        check_vma=False,
    )
```

```python
import functools

import jax
import jax.numpy as jnp
from jax import lax
from jax.experimental import pallas as pl
from jax.experimental.pallas import tpu as pltpu
from jax.sharding import PartitionSpec as P

F32, BF16, I32 = jnp.float32, jnp.bfloat16, jnp.int32
VMEM_LIMIT = 62 * 1024 * 1024


def whole(memory_space=pltpu.VMEM):
    return pl.BlockSpec(memory_space=memory_space)


def earlier(tokens):
    row = lax.broadcasted_iota(I32, (tokens, tokens), 0)
    column = lax.broadcasted_iota(I32, (tokens, tokens), 1)
    return (row < column).astype(F32).astype(BF16)


def pack_kernel(experts, capacity, ids_ref, gates_ref, hidden_ref, out_ref, place_ref, table, select):
    top_count, tokens = ids_ref.shape
    expert = lax.broadcasted_iota(I32, (experts, tokens), 0)
    named = jnp.zeros((experts, tokens), F32)
    for k in range(top_count):
        named = named + (ids_ref[k : k + 1, :] == expert).astype(F32)
    rank = jnp.dot(named.astype(BF16), earlier(tokens), preferred_element_type=F32).astype(I32)
    target = expert * capacity + rank
    for k in range(top_count):
        place_ref[k : k + 1, :] = jnp.sum(
            jnp.where(ids_ref[k : k + 1, :] == expert, target, 0), axis=0, keepdims=True
        )
        table[k * tokens : (k + 1) * tokens, :] = hidden_ref[k]
    rows = out_ref.shape[0]
    step = 128
    for first in range(0, rows, step):
        row = lax.broadcasted_iota(I32, (step, tokens), 0) + first
        for k in range(top_count):
            select[:, k * tokens : (k + 1) * tokens] = jnp.where(
                place_ref[k : k + 1, :] == row, gates_ref[k : k + 1, :].astype(F32), 0.0
            ).astype(BF16)
        out_ref[first : first + step, :] = jnp.dot(
            select[...], table[...], preferred_element_type=F32
        ).astype(BF16)


def pack(ids_t, gates_t, hidden_t, experts, capacity):
    top_count, tokens, hidden_units = hidden_t.shape
    return pl.pallas_call(
        functools.partial(pack_kernel, experts, capacity),
        out_shape=(
            jax.ShapeDtypeStruct((experts * capacity, hidden_units), BF16),
            jax.ShapeDtypeStruct((top_count, tokens), I32),
        ),
        in_specs=[whole()] * 3,
        out_specs=(whole(), whole()),
        scratch_shapes=[
            pltpu.VMEM((top_count * tokens, hidden_units), BF16),
            pltpu.VMEM((128, top_count * tokens), BF16),
        ],
        compiler_params=pltpu.CompilerParams(vmem_limit_bytes=VMEM_LIMIT),
        name="pack",
    )(ids_t, gates_t, hidden_t)


def source_rank(ids, expert, tokens):
    named = jnp.max((ids == expert).astype(F32), axis=0, keepdims=True)
    rank = jnp.dot(named.astype(BF16), earlier(tokens), preferred_element_type=F32)
    return jnp.where(named > 0.5, rank.astype(I32), -1)


def upstream_kernel(capacity, expert_ref, ids_ref, grad_ref, weight_ref, out_ref):
    tokens = grad_ref.shape[0]
    dense = lax.dot_general(
        grad_ref[...], weight_ref[...], (((1,), (1,)), ((), ())), preferred_element_type=F32
    ).astype(BF16)
    rank = source_rank(ids_ref[0], expert_ref[0], tokens)
    choose = (rank == lax.broadcasted_iota(I32, (capacity, tokens), 0)).astype(F32).astype(BF16)
    out_ref[0] = jnp.dot(choose, dense, preferred_element_type=F32).astype(BF16)


def upstream(expert, ids_all, grads, weight, capacity):
    sources, top_count, tokens = ids_all.shape
    hidden_units, width = weight.shape
    return pl.pallas_call(
        functools.partial(upstream_kernel, capacity),
        out_shape=jax.ShapeDtypeStruct((sources, capacity, hidden_units), BF16),
        grid_spec=pltpu.PrefetchScalarGridSpec(
            num_scalar_prefetch=1,
            grid=(sources,),
            in_specs=[
                pl.BlockSpec((1, top_count, tokens), lambda j, e: (j, 0, 0)),
                pl.BlockSpec((tokens, width), lambda j, e: (j, 0)),
                pl.BlockSpec((hidden_units, width), lambda j, e: (0, 0)),
            ],
            out_specs=pl.BlockSpec((1, capacity, hidden_units), lambda j, e: (j, 0, 0)),
        ),
        compiler_params=pltpu.CompilerParams(vmem_limit_bytes=VMEM_LIMIT),
        name="upstream",
    )(expert, ids_all, grads, weight)


def weight_kernel(scalar_ref, ids_ref, hidden_ref, grad_ref, out_ref, dense):
    sources, top_count, tokens = ids_ref.shape
    capacity = hidden_ref.shape[1]

    @pl.when(pl.program_id(0) == 0)
    def _():
        for j in range(sources):
            rank = source_rank(ids_ref[j], scalar_ref[0], tokens)
            choose = (rank == lax.broadcasted_iota(I32, (capacity, tokens), 0)).astype(F32).astype(BF16)
            dense[:, j * tokens : (j + 1) * tokens] = lax.dot_general(
                hidden_ref[j], choose, (((0,), (0,)), ((), ())), preferred_element_type=F32
            ).astype(BF16)

    total = jnp.dot(dense[...], grad_ref[...], preferred_element_type=F32)
    out_ref[...] = (total * scalar_ref[1].astype(F32)).astype(BF16)


def weight_sum(scalars, ids_all, recv_hidden, grads):
    sources, capacity, hidden_units = recv_hidden.shape
    _, top_count, tokens = ids_all.shape
    rows, width = grads.shape
    step = 256
    return pl.pallas_call(
        weight_kernel,
        out_shape=jax.ShapeDtypeStruct((hidden_units, width), BF16),
        grid_spec=pltpu.PrefetchScalarGridSpec(
            num_scalar_prefetch=1,
            grid=(width // step,),
            in_specs=[
                pl.BlockSpec((sources, top_count, tokens), lambda n, e: (0, 0, 0)),
                pl.BlockSpec((sources, capacity, hidden_units), lambda n, e: (0, 0, 0)),
                pl.BlockSpec((rows, step), lambda n, e: (0, n)),
            ],
            out_specs=pl.BlockSpec((hidden_units, step), lambda n, e: (0, n)),
            scratch_shapes=[pltpu.VMEM((hidden_units, rows), BF16)],
        ),
        compiler_params=pltpu.CompilerParams(vmem_limit_bytes=VMEM_LIMIT),
        name="weight_sum",
    )(scalars, ids_all, recv_hidden, grads)


RING = 8
ID_ROWS = 8
PARTS = 4
UNPACK_FLOPS = 40_000_000_000
OFFSETS = (0, -1, 1, -2, 2, -3, 3, 4)
SWAP = [(i, i ^ 1) for i in range(16)]


def ring_device(position, core):
    z, y = (position, 0) if position < 4 else (7 - position, 1)
    return (z * 2 + y) * 2 + core


def ring_shift(step):
    return [
        (ring_device(p, core), ring_device((p + step) % RING, core))
        for p in range(RING)
        for core in range(2)
    ]


def ring_position(device):
    z, y = device >> 2, (device >> 1) & 1
    return jnp.where(y == 0, z, 7 - z)


def ring_pack_kernel(capacity, me_ref, ids_ref, gates_ref, hidden_ref, *rest):
    outs, (place_ref, table, select, blocks, sems) = rest[:RING], rest[RING:]
    top_count, tokens = ids_ref.shape
    experts = 2 * RING
    expert = lax.broadcasted_iota(I32, (experts, tokens), 0)
    named = jnp.zeros((experts, tokens), F32)
    for k in range(top_count):
        named = named + (ids_ref[k : k + 1, :] == expert).astype(F32)
    rank = jnp.dot(named.astype(BF16), earlier(tokens), preferred_element_type=F32).astype(I32)
    me = me_ref[0]
    target = (ring_position(expert) * 2 + ((expert & 1) ^ (me & 1))) * capacity + rank
    for k in range(top_count):
        place_ref[k : k + 1, :] = jnp.sum(
            jnp.where(ids_ref[k : k + 1, :] == expert, target, 0), axis=0, keepdims=True
        )
        table[k * tokens : (k + 1) * tokens, :] = hidden_ref[k]
    step = 2 * capacity
    copies = []
    for d in range(RING):
        row = lax.broadcasted_iota(I32, (step, tokens), 0) + ((ring_position(me) + d) & 7) * step
        for k in range(top_count):
            select[:, k * tokens : (k + 1) * tokens] = jnp.where(
                place_ref[k : k + 1, :] == row, gates_ref[k : k + 1, :].astype(F32), 0.0
            ).astype(BF16)
        blocks[d] = jnp.dot(select[...], table[...], preferred_element_type=F32).astype(BF16)
        copies.append(pltpu.make_async_copy(blocks.at[d], outs[d], sems.at[d]))
        copies[-1].start()
    for copy in copies:
        copy.wait()


def ring_pack(me, ids_t, gates_t, hidden_t, capacity):
    top_count, tokens, hidden_units = hidden_t.shape
    block = jax.ShapeDtypeStruct((2 * capacity, hidden_units), BF16)
    *blocks, place = pl.pallas_call(
        functools.partial(ring_pack_kernel, capacity),
        out_shape=(block,) * RING + (jax.ShapeDtypeStruct((top_count, tokens), I32),),
        in_specs=[whole(pltpu.SMEM)] + [whole()] * 3,
        out_specs=(whole(pltpu.HBM),) * RING + (whole(),),
        scratch_shapes=[
            pltpu.VMEM((top_count * tokens, hidden_units), BF16),
            pltpu.VMEM((2 * capacity, top_count * tokens), BF16),
            pltpu.VMEM((RING, 2 * capacity, hidden_units), BF16),
            pltpu.SemaphoreType.DMA((RING,)),
        ],
        compiler_params=pltpu.CompilerParams(vmem_limit_bytes=VMEM_LIMIT),
        cost_estimate=pl.CostEstimate(flops=3_000_000_000, bytes_accessed=5_000_000, transcendentals=0),
        name="pack",
    )(me, ids_t, gates_t, hidden_t)
    return blocks, place


def both_ranks(ids, me, capacity, tokens):
    own = source_rank(ids, me, tokens)
    other = source_rank(ids, me ^ 1, tokens)
    return own, jnp.where(other >= 0, other + capacity, -1)


def load(refs, buffer, sems, first):
    copies, at = [], 0
    for n, ref in enumerate(refs):
        copies.append(
            pltpu.make_async_copy(ref, buffer.at[pl.ds(at, ref.shape[0])], sems.at[first + n])
        )
        copies[-1].start()
        at += ref.shape[0]
    return copies


def load_pieces(refs, grads, ids, sems, first):
    tokens = ids.shape[2]
    rows, routes, at = [], [], 0
    for n, ref in enumerate(refs):
        extra = ref.shape[0] % 16
        count = ref.shape[0] - extra
        rows.append(
            pltpu.make_async_copy(
                ref.at[pl.ds(0, count)], grads.at[pl.ds(at, count)], sems.at[first + 2 * n]
            )
        )
        at += count
        if extra:
            routes.append(
                pltpu.make_async_copy(
                    ref.at[pl.ds(count, extra), pl.ds(0, tokens)],
                    ids.at[at // tokens - 1],
                    sems.at[first + 2 * n + 1],
                )
            )
    for copy in routes + rows:
        copy.start()
    return routes, rows


def ring_upstream_kernel(capacity, offsets, pieces, me_ref, own_ref, other_ref, *rest):
    blocks = len(offsets)
    grad_refs, (out_ref, weights, grads, ids, dense, rows, sems, out_sems) = rest[:pieces], rest[-8:]
    tokens = ids.shape[2]
    me = me_ref[0]
    routes, loads = load_pieces(grad_refs, grads, ids, sems, 2)
    loads += routes
    weight_loads = [
        pltpu.make_async_copy(own_ref, weights.at[0], sems.at[0]),
        pltpu.make_async_copy(other_ref, weights.at[1], sems.at[1]),
    ]
    for copy in weight_loads:
        copy.start()
    for copy in loads:
        copy.wait()
    for i in range(2):
        weight_loads[i].wait()
        product = lax.dot_general(
            grads[...], weights[i], (((1,), (1,)), ((), ())), preferred_element_type=F32
        ).astype(BF16)
        for b in range(blocks):
            dense[b, i * tokens : (i + 1) * tokens, :] = product[b * tokens : (b + 1) * tokens, :]
    row = lax.broadcasted_iota(I32, (2 * capacity, 2 * tokens), 0)
    copies = []
    for b, offset in enumerate(offsets):
        ranks = both_ranks(ids[b].astype(F32).astype(I32), me, capacity, tokens)
        choose = (jnp.concatenate(ranks, axis=1) == row).astype(F32).astype(BF16)
        rows[b] = jnp.dot(choose, dense[b], preferred_element_type=F32).astype(BF16)
        goal = out_ref.at[(ring_position(me) + offset + RING) & 7]
        copies.append(pltpu.make_async_copy(rows.at[b], goal, out_sems.at[b]))
        copies[-1].start()
    for copy in copies:
        copy.wait()


def ring_upstream(me, tokens, offsets, pieces, so_far, own_weight, other_weight, capacity):
    hidden_units, width = own_weight.shape
    blocks = len(offsets)
    return pl.pallas_call(
        functools.partial(ring_upstream_kernel, capacity, offsets, len(pieces)),
        out_shape=jax.ShapeDtypeStruct((RING, 2 * capacity, hidden_units), BF16),
        in_specs=[whole(pltpu.SMEM)] + [whole(pltpu.HBM)] * (2 + len(pieces) + len(so_far)),
        out_specs=whole(pltpu.HBM),
        input_output_aliases={3 + len(pieces): 0} if so_far else {},
        scratch_shapes=[
            pltpu.VMEM((2, hidden_units, width), BF16),
            pltpu.VMEM((blocks * tokens, width), BF16),
            pltpu.VMEM((blocks, ID_ROWS, tokens), BF16),
            pltpu.VMEM((blocks, 2 * tokens, hidden_units), BF16),
            pltpu.VMEM((blocks, 2 * capacity, hidden_units), BF16),
            pltpu.SemaphoreType.DMA((2 + 2 * len(pieces),)),
            pltpu.SemaphoreType.DMA((blocks,)),
        ],
        compiler_params=pltpu.CompilerParams(vmem_limit_bytes=VMEM_LIMIT),
        cost_estimate=pl.CostEstimate(
            flops=4 * blocks * tokens * hidden_units * width,
            bytes_accessed=2 * (blocks * tokens + 2 * hidden_units) * width,
            transcendentals=0,
        ),
        name="upstream",
    )(me, own_weight, other_weight, *pieces, *so_far)


def ring_weight_kernel(capacity, other, pieces, me_ref, *rest):
    grad_refs, hidden_refs = rest[:pieces], rest[pieces : pieces + RING]
    outs, (grads, ids, hidden, dense, sems) = rest[pieces + RING : -5], rest[-5:]
    tokens = ids.shape[2]
    me = me_ref[0]
    routes, grad_loads = load_pieces(grad_refs, grads, ids, sems, 0)
    loads = [
        pltpu.make_async_copy(ref, hidden.at[q], sems.at[2 * pieces + q])
        for q, ref in enumerate(hidden_refs)
    ]
    for copy in loads:
        copy.start()
    for copy in routes + loads:
        copy.wait()
    row = lax.broadcasted_iota(I32, (2 * capacity, tokens), 0)
    for q in range(RING):
        rank = both_ranks(ids[q].astype(F32).astype(I32), me, capacity, tokens)[other]
        choose = (rank == row).astype(F32).astype(BF16)
        dense[:, q * tokens : (q + 1) * tokens] = lax.dot_general(
            hidden[q], choose, (((0,), (0,)), ((), ())), preferred_element_type=F32
        ).astype(BF16)
    for copy in grad_loads:
        copy.wait()
    width = grads.shape[1]
    step = 256

    @pl.loop(0, width // step)
    def _(n):
        at = pl.ds(pl.multiple_of(n * step, step), step)
        total = jnp.dot(dense[...], grads[:, at], preferred_element_type=F32)
        height = total.shape[0] // len(outs)
        for part, part_ref in enumerate(outs):
            part_ref[:, at] = total[part * height : (part + 1) * height].astype(BF16)


def ring_weight_sum(me, tokens, pieces, hidden, other, capacity):
    width = pieces[0].shape[1]
    hidden_units = hidden[0].shape[1]
    result = jax.ShapeDtypeStruct((hidden_units // PARTS, width), BF16)
    return pl.pallas_call(
        functools.partial(ring_weight_kernel, capacity, other, len(pieces)),
        out_shape=(result,) * PARTS,
        in_specs=[whole(pltpu.SMEM)] + [whole(pltpu.HBM)] * (len(pieces) + RING),
        out_specs=(whole(),) * PARTS,
        scratch_shapes=[
            pltpu.VMEM((RING * tokens, width), BF16),
            pltpu.VMEM((RING, ID_ROWS, tokens), BF16),
            pltpu.VMEM((RING, 2 * capacity, hidden_units), BF16),
            pltpu.VMEM((hidden_units, RING * tokens), BF16),
            pltpu.SemaphoreType.DMA((2 * len(pieces) + RING,)),
        ],
        compiler_params=pltpu.CompilerParams(vmem_limit_bytes=VMEM_LIMIT),
        cost_estimate=pl.CostEstimate(flops=1_000_000, bytes_accessed=1_000_000, transcendentals=0),
        name="weight_other" if other else "weight_own",
    )(me, *pieces, *hidden)


def add_kernel(trained_ref, *rest):
    parts = len(rest) // 2
    own_refs, came_refs, out_ref = rest[:parts], rest[parts : 2 * parts], rest[-1]
    trained, at = trained_ref[0].astype(F32), 0
    for own_ref, came_ref in zip(own_refs, came_refs):
        height = own_ref.shape[0]
        total = own_ref[...].astype(F32) + came_ref[...].astype(F32)
        out_ref[at : at + height, :] = (total * trained).astype(BF16)
        at += height


def add_parts(trained, own, came):
    height, width = own[0].shape
    step = 512
    part = pl.BlockSpec((height, step), lambda n: (0, n))
    rows = height * len(own)
    return pl.pallas_call(
        add_kernel,
        out_shape=jax.ShapeDtypeStruct((rows, width), BF16),
        grid=(width // step,),
        in_specs=[whole(pltpu.SMEM)] + [part] * (2 * len(own)),
        out_specs=pl.BlockSpec((rows, step), lambda n: (0, n)),
        compiler_params=pltpu.CompilerParams(vmem_limit_bytes=VMEM_LIMIT),
        cost_estimate=pl.CostEstimate(flops=1_000_000, bytes_accessed=1_000_000, transcendentals=0),
        name="weight_add",
    )(trained, *own, *came)


def unpack_kernel(place_ref, gates_ref, hidden_ref, *rest):
    back_refs, (grad_ref, gate_ref, select, sums, back, sems) = rest[:-6], rest[-6:]
    tokens, top_count = place_ref.shape
    rows = back.shape[0]
    copies = load(back_refs, back, sems, 0)
    lane = lax.broadcasted_iota(I32, (tokens, rows), 1)
    for k in range(top_count):
        select[k * tokens : (k + 1) * tokens, :] = (
            (place_ref[:, k : k + 1] == lane).astype(F32).astype(BF16)
        )
    sums[...] = jnp.zeros_like(sums)
    for copy in copies:
        copy.wait()
    up = jnp.dot(select[...], back[...], preferred_element_type=F32)
    for k in range(top_count):
        mine = up[k * tokens : (k + 1) * tokens, :]
        grad_ref[k] = (gates_ref[:, k : k + 1].astype(F32) * mine).astype(BF16)
        sums[:, k : k + 1] = jnp.sum(hidden_ref[k].astype(F32) * mine, axis=1, keepdims=True)
    gate_ref[...] = sums[...].T[:top_count, :].astype(BF16)


def unpack(place, gates, hidden_t, back):
    top_count, tokens, hidden_units = hidden_t.shape
    rows = sum(block.shape[0] for block in back)
    return pl.pallas_call(
        unpack_kernel,
        out_shape=(
            jax.ShapeDtypeStruct((top_count, tokens, hidden_units), BF16),
            jax.ShapeDtypeStruct((top_count, tokens), BF16),
        ),
        in_specs=[whole()] * 3 + [whole(pltpu.HBM)] * len(back),
        out_specs=(whole(), whole()),
        scratch_shapes=[
            pltpu.VMEM((top_count * tokens, rows), BF16),
            pltpu.VMEM((tokens, 128), F32),
            pltpu.VMEM((rows, hidden_units), BF16),
            pltpu.SemaphoreType.DMA((len(back),)),
        ],
        compiler_params=pltpu.CompilerParams(vmem_limit_bytes=VMEM_LIMIT),
        cost_estimate=pl.CostEstimate(
            flops=UNPACK_FLOPS, bytes_accessed=6 * rows * hidden_units, transcendentals=0
        ),
        name="unpack",
    )(place, gates, hidden_t, *back)


def ring_exchange(out_grad, hidden_t, ids_t, gates_t, scalars, weight, capacity):
    def send(value, step):
        return lax.ppermute(value, "expert", ring_shift(step))

    me = scalars[:1]
    tokens, width = out_grad.shape
    half = tokens // 2
    spare = ((0, ID_ROWS - ids_t.shape[0]), (0, width - tokens))
    block = jnp.concatenate([out_grad, jnp.pad(ids_t.astype(BF16), spare, constant_values=-1)])
    packed, place = ring_pack(me, ids_t, gates_t, hidden_t, capacity)
    other_weight = lax.ppermute(weight, "expert", SWAP)
    barrier = lax.optimization_barrier
    hidden = [None] * RING

    def send_hidden(*chosen):
        for q in chosen:
            hidden[q] = send(packed[-OFFSETS[q] % RING], -OFFSETS[q] % RING)

    ahead, behind = send(block, 1), send(block, -1)
    ahead, behind, *packed = barrier((ahead, behind, *packed))
    pieces = [block, ahead, behind]
    hidden[0] = packed[0]
    ahead, behind = send(ahead, 1), send(behind, -1)
    ahead, behind, other_weight = barrier((ahead, behind, other_weight))
    pieces += [ahead, behind]
    upstream_of = functools.partial(
        ring_upstream, me, tokens, own_weight=weight, other_weight=other_weight, capacity=capacity
    )
    ahead, behind = send(ahead, 1), send(behind, -1)
    send_hidden(3, 4)
    up = upstream_of(OFFSETS[:5], pieces[:5], ())
    ahead, behind, hidden[3], hidden[4], up = barrier((ahead, behind, hidden[3], hidden[4], up))
    pieces += [ahead, behind]
    pieces += [send(ahead[:half], 1), send(behind[half:], -1)]
    send_hidden(5, 6, 7, 1, 2)
    up = upstream_of(OFFSETS[5:], pieces[5:], (up,))
    *hidden, up = barrier((*hidden, up))
    groups = [[ring_device(p, core) for p in range(RING)] for core in range(2)]
    back = lax.all_to_all(up, "expert", 0, 0, axis_index_groups=groups, tiled=True)
    theirs = ring_weight_sum(me, tokens, pieces, hidden, True, capacity)
    came = [lax.ppermute(part, "expert", SWAP) for part in theirs]
    own = ring_weight_sum(me, tokens, pieces, hidden, False, capacity)
    weight_grad = add_parts(scalars[1:], own, came)
    place, weight_grad = barrier((place, weight_grad))
    return place, [back.reshape(-1, back.shape[2])], weight_grad


def gather_exchange(out_grad, hidden_t, ids_t, gates_t, scalars, weight, capacity):
    experts = lax.axis_size("expert")
    hidden_units = weight.shape[0]
    ids_all = lax.all_gather(ids_t, "expert", axis=0)
    packed, place = pack(ids_t, gates_t, hidden_t, experts, capacity)
    grads = lax.all_gather(out_grad, "expert", axis=0, tiled=True)
    recv_hidden = lax.all_to_all(
        packed.reshape(experts, capacity, hidden_units), "expert", 0, 0, tiled=True
    )
    up = upstream(scalars[:1], ids_all, grads, weight, capacity)
    back = lax.all_to_all(up, "expert", 0, 0, tiled=True)
    weight_grad = weight_sum(scalars, ids_all, recv_hidden, grads)
    return place, [back.reshape(experts * capacity, hidden_units)], weight_grad


def local(out_grad, saved_hidden, expert_ids, gate_weights, trained, down_weight):
    experts = lax.axis_size("expert")
    tokens, top_count, _ = saved_hidden.shape
    capacity = min(tokens, 3 * tokens * top_count // (2 * experts))
    hidden_t = saved_hidden.transpose(1, 0, 2)
    scalars = jnp.stack([lax.axis_index("expert").astype(I32), trained[0]])
    exchange = ring_exchange if experts == 2 * RING else gather_exchange
    place, back, weight_grad = exchange(
        out_grad, hidden_t, expert_ids.T, gate_weights.T, scalars, down_weight[0], capacity
    )
    hidden_grad, gate_grad = unpack(place.T, gate_weights, hidden_t, back)
    return hidden_grad.transpose(1, 0, 2), gate_grad.T, weight_grad[None]


def solution(mesh):
    placed = (
        P(("groups", "expert"), None),
        P(("groups", "expert"), None, None),
        P(("groups", "expert"), None),
        P(("groups", "expert"), None),
        P(("groups", "expert")),
        P("expert", None, None),
    )
    return jax.shard_map(
        local,
        mesh=mesh,
        in_specs=placed,
        out_specs=(
            P(("groups", "expert"), None, None),
            P(("groups", "expert"), None),
            P(("groups", "expert"), None, None),
        ),
        check_vma=False,
    )
```

```python
import functools

import jax
import jax.numpy as jnp
from jax import lax
from jax.experimental import pallas as pl
from jax.experimental.pallas import tpu as pltpu
from jax.sharding import PartitionSpec as P

F32, BF16, I32 = jnp.float32, jnp.bfloat16, jnp.int32
VMEM_LIMIT = 62 * 1024 * 1024


def whole(memory_space=pltpu.VMEM):
    return pl.BlockSpec(memory_space=memory_space)


def earlier(tokens):
    row = lax.broadcasted_iota(I32, (tokens, tokens), 0)
    column = lax.broadcasted_iota(I32, (tokens, tokens), 1)
    return (row < column).astype(F32).astype(BF16)


def pack_kernel(experts, capacity, ids_ref, gates_ref, hidden_ref, out_ref, place_ref, table, select):
    top_count, tokens = ids_ref.shape
    expert = lax.broadcasted_iota(I32, (experts, tokens), 0)
    named = jnp.zeros((experts, tokens), F32)
    for k in range(top_count):
        named = named + (ids_ref[k : k + 1, :] == expert).astype(F32)
    rank = jnp.dot(named.astype(BF16), earlier(tokens), preferred_element_type=F32).astype(I32)
    target = expert * capacity + rank
    for k in range(top_count):
        place_ref[k : k + 1, :] = jnp.sum(
            jnp.where(ids_ref[k : k + 1, :] == expert, target, 0), axis=0, keepdims=True
        )
        table[k * tokens : (k + 1) * tokens, :] = hidden_ref[k]
    rows = out_ref.shape[0]
    step = 128
    for first in range(0, rows, step):
        row = lax.broadcasted_iota(I32, (step, tokens), 0) + first
        for k in range(top_count):
            select[:, k * tokens : (k + 1) * tokens] = jnp.where(
                place_ref[k : k + 1, :] == row, gates_ref[k : k + 1, :].astype(F32), 0.0
            ).astype(BF16)
        out_ref[first : first + step, :] = jnp.dot(
            select[...], table[...], preferred_element_type=F32
        ).astype(BF16)


def pack(ids_t, gates_t, hidden_t, experts, capacity):
    top_count, tokens, hidden_units = hidden_t.shape
    return pl.pallas_call(
        functools.partial(pack_kernel, experts, capacity),
        out_shape=(
            jax.ShapeDtypeStruct((experts * capacity, hidden_units), BF16),
            jax.ShapeDtypeStruct((top_count, tokens), I32),
        ),
        in_specs=[whole()] * 3,
        out_specs=(whole(), whole()),
        scratch_shapes=[
            pltpu.VMEM((top_count * tokens, hidden_units), BF16),
            pltpu.VMEM((128, top_count * tokens), BF16),
        ],
        compiler_params=pltpu.CompilerParams(vmem_limit_bytes=VMEM_LIMIT),
        name="pack",
    )(ids_t, gates_t, hidden_t)


def source_rank(ids, expert, tokens):
    named = jnp.max((ids == expert).astype(F32), axis=0, keepdims=True)
    rank = jnp.dot(named.astype(BF16), earlier(tokens), preferred_element_type=F32)
    return jnp.where(named > 0.5, rank.astype(I32), -1)


def upstream_kernel(capacity, expert_ref, ids_ref, grad_ref, weight_ref, out_ref):
    tokens = grad_ref.shape[0]
    dense = lax.dot_general(
        grad_ref[...], weight_ref[...], (((1,), (1,)), ((), ())), preferred_element_type=F32
    ).astype(BF16)
    rank = source_rank(ids_ref[0], expert_ref[0], tokens)
    choose = (rank == lax.broadcasted_iota(I32, (capacity, tokens), 0)).astype(F32).astype(BF16)
    out_ref[0] = jnp.dot(choose, dense, preferred_element_type=F32).astype(BF16)


def upstream(expert, ids_all, grads, weight, capacity):
    sources, top_count, tokens = ids_all.shape
    hidden_units, width = weight.shape
    return pl.pallas_call(
        functools.partial(upstream_kernel, capacity),
        out_shape=jax.ShapeDtypeStruct((sources, capacity, hidden_units), BF16),
        grid_spec=pltpu.PrefetchScalarGridSpec(
            num_scalar_prefetch=1,
            grid=(sources,),
            in_specs=[
                pl.BlockSpec((1, top_count, tokens), lambda j, e: (j, 0, 0)),
                pl.BlockSpec((tokens, width), lambda j, e: (j, 0)),
                pl.BlockSpec((hidden_units, width), lambda j, e: (0, 0)),
            ],
            out_specs=pl.BlockSpec((1, capacity, hidden_units), lambda j, e: (j, 0, 0)),
        ),
        compiler_params=pltpu.CompilerParams(vmem_limit_bytes=VMEM_LIMIT),
        name="upstream",
    )(expert, ids_all, grads, weight)


def weight_kernel(scalar_ref, ids_ref, hidden_ref, grad_ref, out_ref, dense):
    sources, top_count, tokens = ids_ref.shape
    capacity = hidden_ref.shape[1]

    @pl.when(pl.program_id(0) == 0)
    def _():
        for j in range(sources):
            rank = source_rank(ids_ref[j], scalar_ref[0], tokens)
            choose = (rank == lax.broadcasted_iota(I32, (capacity, tokens), 0)).astype(F32).astype(BF16)
            dense[:, j * tokens : (j + 1) * tokens] = lax.dot_general(
                hidden_ref[j], choose, (((0,), (0,)), ((), ())), preferred_element_type=F32
            ).astype(BF16)

    total = jnp.dot(dense[...], grad_ref[...], preferred_element_type=F32)
    out_ref[...] = (total * scalar_ref[1].astype(F32)).astype(BF16)


def weight_sum(scalars, ids_all, recv_hidden, grads):
    sources, capacity, hidden_units = recv_hidden.shape
    _, top_count, tokens = ids_all.shape
    rows, width = grads.shape
    step = 256
    return pl.pallas_call(
        weight_kernel,
        out_shape=jax.ShapeDtypeStruct((hidden_units, width), BF16),
        grid_spec=pltpu.PrefetchScalarGridSpec(
            num_scalar_prefetch=1,
            grid=(width // step,),
            in_specs=[
                pl.BlockSpec((sources, top_count, tokens), lambda n, e: (0, 0, 0)),
                pl.BlockSpec((sources, capacity, hidden_units), lambda n, e: (0, 0, 0)),
                pl.BlockSpec((rows, step), lambda n, e: (0, n)),
            ],
            out_specs=pl.BlockSpec((hidden_units, step), lambda n, e: (0, n)),
            scratch_shapes=[pltpu.VMEM((hidden_units, rows), BF16)],
        ),
        compiler_params=pltpu.CompilerParams(vmem_limit_bytes=VMEM_LIMIT),
        name="weight_sum",
    )(scalars, ids_all, recv_hidden, grads)


RING = 8
ADD_LIMIT = 24 * 1024 * 1024
ID_ROWS = 8
PARTS = 4
UNPACK_FLOPS = 40_000_000_000
OFFSETS = (0, -1, 1, -2, 2, -3, 3, 4)
SWAP = [(i, i ^ 1) for i in range(16)]


def ring_device(position, core):
    z, y = (position, 0) if position < 4 else (7 - position, 1)
    return (z * 2 + y) * 2 + core


def ring_shift(step):
    return [
        (ring_device(p, core), ring_device((p + step) % RING, core))
        for p in range(RING)
        for core in range(2)
    ]


def ring_position(device):
    z, y = device >> 2, (device >> 1) & 1
    return jnp.where(y == 0, z, 7 - z)


def ring_pack_kernel(capacity, me_ref, ids_ref, gates_ref, hidden_ref, *rest):
    outs, (place_ref, table, select, blocks, sems) = rest[:RING], rest[RING:]
    top_count, tokens = ids_ref.shape
    experts = 2 * RING
    expert = lax.broadcasted_iota(I32, (experts, tokens), 0)
    named = jnp.zeros((experts, tokens), F32)
    for k in range(top_count):
        named = named + (ids_ref[k : k + 1, :] == expert).astype(F32)
    rank = jnp.dot(named.astype(BF16), earlier(tokens), preferred_element_type=F32).astype(I32)
    me = me_ref[0]
    target = (ring_position(expert) * 2 + ((expert & 1) ^ (me & 1))) * capacity + rank
    for k in range(top_count):
        place_ref[k : k + 1, :] = jnp.sum(
            jnp.where(ids_ref[k : k + 1, :] == expert, target, 0), axis=0, keepdims=True
        )
        table[k * tokens : (k + 1) * tokens, :] = hidden_ref[k]
    step = 2 * capacity
    copies = []
    for d in range(RING):
        row = lax.broadcasted_iota(I32, (step, tokens), 0) + ((ring_position(me) + d) & 7) * step
        for k in range(top_count):
            select[:, k * tokens : (k + 1) * tokens] = jnp.where(
                place_ref[k : k + 1, :] == row, gates_ref[k : k + 1, :].astype(F32), 0.0
            ).astype(BF16)
        blocks[d] = jnp.dot(select[...], table[...], preferred_element_type=F32).astype(BF16)
        copies.append(pltpu.make_async_copy(blocks.at[d], outs[d], sems.at[d]))
        copies[-1].start()
    for copy in copies:
        copy.wait()


def ring_pack(me, ids_t, gates_t, hidden_t, capacity):
    top_count, tokens, hidden_units = hidden_t.shape
    block = jax.ShapeDtypeStruct((2 * capacity, hidden_units), BF16)
    *blocks, place = pl.pallas_call(
        functools.partial(ring_pack_kernel, capacity),
        out_shape=(block,) * RING + (jax.ShapeDtypeStruct((top_count, tokens), I32),),
        in_specs=[whole(pltpu.SMEM)] + [whole()] * 3,
        out_specs=(whole(pltpu.HBM),) * RING + (whole(),),
        scratch_shapes=[
            pltpu.VMEM((top_count * tokens, hidden_units), BF16),
            pltpu.VMEM((2 * capacity, top_count * tokens), BF16),
            pltpu.VMEM((RING, 2 * capacity, hidden_units), BF16),
            pltpu.SemaphoreType.DMA((RING,)),
        ],
        compiler_params=pltpu.CompilerParams(vmem_limit_bytes=VMEM_LIMIT),
        cost_estimate=pl.CostEstimate(flops=3_000_000_000, bytes_accessed=5_000_000, transcendentals=0),
        name="pack",
    )(me, ids_t, gates_t, hidden_t)
    return blocks, place


def both_ranks(ids, me, capacity, tokens):
    own = source_rank(ids, me, tokens)
    other = source_rank(ids, me ^ 1, tokens)
    return own, jnp.where(other >= 0, other + capacity, -1)


def load(refs, buffer, sems, first):
    copies, at = [], 0
    for n, ref in enumerate(refs):
        copies.append(
            pltpu.make_async_copy(ref, buffer.at[pl.ds(at, ref.shape[0])], sems.at[first + n])
        )
        copies[-1].start()
        at += ref.shape[0]
    return copies


def load_pieces(refs, grads, ids, sems, first):
    tokens = ids.shape[2]
    rows, routes, at = [], [], 0
    for n, ref in enumerate(refs):
        extra = ref.shape[0] % 16
        count = ref.shape[0] - extra
        rows.append(
            pltpu.make_async_copy(
                ref.at[pl.ds(0, count)], grads.at[pl.ds(at, count)], sems.at[first + 2 * n]
            )
        )
        at += count
        if extra:
            routes.append(
                pltpu.make_async_copy(
                    ref.at[pl.ds(count, extra), pl.ds(0, tokens)],
                    ids.at[at // tokens - 1],
                    sems.at[first + 2 * n + 1],
                )
            )
    for copy in routes + rows:
        copy.start()
    return routes, rows


def ring_upstream_kernel(capacity, offsets, pieces, me_ref, own_ref, other_ref, *rest):
    blocks = len(offsets)
    grad_refs, (out_ref, weights, grads, ids, dense, rows, sems, out_sems) = rest[:pieces], rest[-8:]
    tokens = ids.shape[2]
    me = me_ref[0]
    routes, loads = load_pieces(grad_refs, grads, ids, sems, 2)
    loads += routes
    weight_loads = [
        pltpu.make_async_copy(own_ref, weights.at[0], sems.at[0]),
        pltpu.make_async_copy(other_ref, weights.at[1], sems.at[1]),
    ]
    for copy in weight_loads:
        copy.start()
    for copy in loads:
        copy.wait()
    for i in range(2):
        weight_loads[i].wait()
        product = lax.dot_general(
            grads[...], weights[i], (((1,), (1,)), ((), ())), preferred_element_type=F32
        ).astype(BF16)
        for b in range(blocks):
            dense[b, i * tokens : (i + 1) * tokens, :] = product[b * tokens : (b + 1) * tokens, :]
    row = lax.broadcasted_iota(I32, (2 * capacity, 2 * tokens), 0)
    copies = []
    for b, offset in enumerate(offsets):
        ranks = both_ranks(ids[b].astype(F32).astype(I32), me, capacity, tokens)
        choose = (jnp.concatenate(ranks, axis=1) == row).astype(F32).astype(BF16)
        rows[b] = jnp.dot(choose, dense[b], preferred_element_type=F32).astype(BF16)
        goal = out_ref.at[(ring_position(me) + offset + RING) & 7]
        copies.append(pltpu.make_async_copy(rows.at[b], goal, out_sems.at[b]))
        copies[-1].start()
    for copy in copies:
        copy.wait()


def ring_upstream(me, tokens, offsets, pieces, so_far, own_weight, other_weight, capacity):
    hidden_units, width = own_weight.shape
    blocks = len(offsets)
    return pl.pallas_call(
        functools.partial(ring_upstream_kernel, capacity, offsets, len(pieces)),
        out_shape=jax.ShapeDtypeStruct((RING, 2 * capacity, hidden_units), BF16),
        in_specs=[whole(pltpu.SMEM)] + [whole(pltpu.HBM)] * (2 + len(pieces) + len(so_far)),
        out_specs=whole(pltpu.HBM),
        input_output_aliases={3 + len(pieces): 0} if so_far else {},
        scratch_shapes=[
            pltpu.VMEM((2, hidden_units, width), BF16),
            pltpu.VMEM((blocks * tokens, width), BF16),
            pltpu.VMEM((blocks, ID_ROWS, tokens), BF16),
            pltpu.VMEM((blocks, 2 * tokens, hidden_units), BF16),
            pltpu.VMEM((blocks, 2 * capacity, hidden_units), BF16),
            pltpu.SemaphoreType.DMA((2 + 2 * len(pieces),)),
            pltpu.SemaphoreType.DMA((blocks,)),
        ],
        compiler_params=pltpu.CompilerParams(vmem_limit_bytes=VMEM_LIMIT),
        cost_estimate=pl.CostEstimate(
            flops=4 * blocks * tokens * hidden_units * width,
            bytes_accessed=2 * (blocks * tokens + 2 * hidden_units) * width,
            transcendentals=0,
        ),
        name="upstream",
    )(me, own_weight, other_weight, *pieces, *so_far)


def ring_weight_kernel(capacity, other, pieces, me_ref, *rest):
    grad_refs, hidden_refs = rest[:pieces], rest[pieces : pieces + RING]
    outs, (grads, ids, hidden, dense, sems) = rest[pieces + RING : -5], rest[-5:]
    tokens = ids.shape[2]
    me = me_ref[0]
    routes, grad_loads = load_pieces(grad_refs, grads, ids, sems, 0)
    loads = [
        pltpu.make_async_copy(ref, hidden.at[q], sems.at[2 * pieces + q])
        for q, ref in enumerate(hidden_refs)
    ]
    for copy in loads:
        copy.start()
    for copy in routes + loads:
        copy.wait()
    row = lax.broadcasted_iota(I32, (2 * capacity, tokens), 0)
    for q in range(RING):
        rank = both_ranks(ids[q].astype(F32).astype(I32), me, capacity, tokens)[other]
        choose = (rank == row).astype(F32).astype(BF16)
        dense[:, q * tokens : (q + 1) * tokens] = lax.dot_general(
            hidden[q], choose, (((0,), (0,)), ((), ())), preferred_element_type=F32
        ).astype(BF16)
    for copy in grad_loads:
        copy.wait()
    width = grads.shape[1]
    step = 512

    @pl.loop(0, width // step)
    def _(n):
        at = pl.ds(pl.multiple_of(n * step, step), step)
        total = jnp.dot(dense[...], grads[:, at], preferred_element_type=F32)
        height = total.shape[0] // len(outs)
        for part, part_ref in enumerate(outs):
            part_ref[:, at] = total[part * height : (part + 1) * height].astype(BF16)


def ring_weight_sum(me, tokens, pieces, hidden, other, capacity):
    width = pieces[0].shape[1]
    hidden_units = hidden[0].shape[1]
    result = jax.ShapeDtypeStruct((hidden_units // PARTS, width), BF16)
    return pl.pallas_call(
        functools.partial(ring_weight_kernel, capacity, other, len(pieces)),
        out_shape=(result,) * PARTS,
        in_specs=[whole(pltpu.SMEM)] + [whole(pltpu.HBM)] * (len(pieces) + RING),
        out_specs=(whole(),) * PARTS,
        scratch_shapes=[
            pltpu.VMEM((RING * tokens, width), BF16),
            pltpu.VMEM((RING, ID_ROWS, tokens), BF16),
            pltpu.VMEM((RING, 2 * capacity, hidden_units), BF16),
            pltpu.VMEM((hidden_units, RING * tokens), BF16),
            pltpu.SemaphoreType.DMA((2 * len(pieces) + RING,)),
        ],
        compiler_params=pltpu.CompilerParams(vmem_limit_bytes=VMEM_LIMIT),
        cost_estimate=pl.CostEstimate(flops=1_000_000, bytes_accessed=1_000_000, transcendentals=0),
        name="weight_other" if other else "weight_own",
    )(me, *pieces, *hidden)


def add_kernel(trained_ref, *rest):
    own_refs, came_refs, (out_ref, own, came, sums, sems) = rest[:PARTS], rest[PARTS : 2 * PARTS], rest[-5:]
    trained = trained_ref[0].astype(F32)
    height = own.shape[1]
    loads = []
    for part in range(PARTS):
        for n, (ref, buffer) in enumerate(((own_refs[part], own), (came_refs[part], came))):
            loads.append(pltpu.make_async_copy(ref, buffer.at[part], sems.at[n, part]))
            loads[-1].start()
    stores = []
    for part in range(PARTS):
        loads[2 * part].wait()
        loads[2 * part + 1].wait()
        total = own[part].astype(F32) + came[part].astype(F32)
        sums[part] = (total * trained).astype(BF16)
        goal = out_ref.at[pl.ds(part * height, height)]
        stores.append(pltpu.make_async_copy(sums.at[part], goal, sems.at[2, part]))
        stores[-1].start()
    for copy in stores:
        copy.wait()


def add_parts(trained, own, came):
    height, width = own[0].shape
    return pl.pallas_call(
        add_kernel,
        out_shape=jax.ShapeDtypeStruct((height * PARTS, width), BF16),
        in_specs=[whole(pltpu.SMEM)] + [whole(pltpu.HBM)] * (2 * PARTS),
        out_specs=whole(pltpu.HBM),
        scratch_shapes=[pltpu.VMEM((PARTS, height, width), BF16)] * 3
        + [pltpu.SemaphoreType.DMA((3, PARTS))],
        compiler_params=pltpu.CompilerParams(vmem_limit_bytes=ADD_LIMIT),
        cost_estimate=pl.CostEstimate(flops=1_000_000, bytes_accessed=1_000_000, transcendentals=0),
        name="weight_add",
    )(trained, *own, *came)


def unpack_kernel(place_ref, gates_ref, hidden_ref, back_ref, grad_ref, gate_ref, select, sums):
    tokens, top_count = place_ref.shape
    rows = back_ref.shape[0]
    lane = lax.broadcasted_iota(I32, (tokens, rows), 1)
    for k in range(top_count):
        select[k * tokens : (k + 1) * tokens, :] = (
            (place_ref[:, k : k + 1] == lane).astype(F32).astype(BF16)
        )
    sums[...] = jnp.zeros_like(sums)
    up = jnp.dot(select[...], back_ref[...], preferred_element_type=F32)
    for k in range(top_count):
        mine = up[k * tokens : (k + 1) * tokens, :]
        grad_ref[k] = (gates_ref[:, k : k + 1].astype(F32) * mine).astype(BF16)
        sums[:, k : k + 1] = jnp.sum(hidden_ref[k].astype(F32) * mine, axis=1, keepdims=True)
    gate_ref[...] = sums[...].T[:top_count, :].astype(BF16)


def unpack(place, gates, hidden_t, back):
    top_count, tokens, hidden_units = hidden_t.shape
    rows = sum(block.shape[0] for block in back)
    return pl.pallas_call(
        unpack_kernel,
        out_shape=(
            jax.ShapeDtypeStruct((top_count, tokens, hidden_units), BF16),
            jax.ShapeDtypeStruct((top_count, tokens), BF16),
        ),
        in_specs=[whole()] * 3 + [whole()] * len(back),
        out_specs=(whole(), whole()),
        scratch_shapes=[
            pltpu.VMEM((top_count * tokens, rows), BF16),
            pltpu.VMEM((tokens, 128), F32),
        ],
        compiler_params=pltpu.CompilerParams(vmem_limit_bytes=24 * 1024 * 1024),
        cost_estimate=pl.CostEstimate(
            flops=UNPACK_FLOPS, bytes_accessed=6 * rows * hidden_units, transcendentals=0
        ),
        name="unpack",
    )(place, gates, hidden_t, *back)


def ring_exchange(out_grad, hidden_t, ids_t, gates_t, scalars, weight, capacity):
    def send(value, step):
        return lax.ppermute(value, "expert", ring_shift(step))

    me = scalars[:1]
    tokens, width = out_grad.shape
    half = tokens // 2
    spare = ((0, ID_ROWS - ids_t.shape[0]), (0, width - tokens))
    block = jnp.concatenate([out_grad, jnp.pad(ids_t.astype(BF16), spare, constant_values=-1)])
    packed, place = ring_pack(me, ids_t, gates_t, hidden_t, capacity)
    other_weight = lax.ppermute(weight, "expert", SWAP)
    barrier = lax.optimization_barrier
    hidden = [None] * RING

    def send_hidden(*chosen):
        for q in chosen:
            hidden[q] = send(packed[-OFFSETS[q] % RING], -OFFSETS[q] % RING)

    ahead, behind = send(block, 1), send(block, -1)
    ahead, behind, *packed = barrier((ahead, behind, *packed))
    pieces = [block, ahead, behind]
    hidden[0] = packed[0]
    ahead, behind = send(ahead, 1), send(behind, -1)
    ahead, behind, other_weight = barrier((ahead, behind, other_weight))
    pieces += [ahead, behind]
    upstream_of = functools.partial(
        ring_upstream, me, tokens, own_weight=weight, other_weight=other_weight, capacity=capacity
    )
    ahead, behind = send(ahead, 1), send(behind, -1)
    send_hidden(3, 4)
    up = upstream_of(OFFSETS[:5], pieces[:5], ())
    ahead, behind, hidden[3], hidden[4], up = barrier((ahead, behind, hidden[3], hidden[4], up))
    pieces += [ahead, behind]
    pieces += [send(ahead[:half], 1), send(behind[half:], -1)]
    send_hidden(5, 6, 7, 1, 2)
    up = upstream_of(OFFSETS[5:], pieces[5:], (up,))
    *hidden, up = barrier((*hidden, up))
    groups = [[ring_device(p, core) for p in range(RING)] for core in range(2)]
    back = lax.all_to_all(up, "expert", 0, 0, axis_index_groups=groups, tiled=True)
    theirs = ring_weight_sum(me, tokens, pieces, hidden, True, capacity)
    came = [lax.ppermute(part, "expert", SWAP) for part in theirs]
    own = ring_weight_sum(me, tokens, pieces, hidden, False, capacity)
    weight_grad = add_parts(scalars[1:], own, came)
    place, weight_grad = barrier((place, weight_grad))
    return place, [back.reshape(-1, back.shape[2])], weight_grad


def gather_exchange(out_grad, hidden_t, ids_t, gates_t, scalars, weight, capacity):
    experts = lax.axis_size("expert")
    hidden_units = weight.shape[0]
    ids_all = lax.all_gather(ids_t, "expert", axis=0)
    packed, place = pack(ids_t, gates_t, hidden_t, experts, capacity)
    grads = lax.all_gather(out_grad, "expert", axis=0, tiled=True)
    recv_hidden = lax.all_to_all(
        packed.reshape(experts, capacity, hidden_units), "expert", 0, 0, tiled=True
    )
    up = upstream(scalars[:1], ids_all, grads, weight, capacity)
    back = lax.all_to_all(up, "expert", 0, 0, tiled=True)
    weight_grad = weight_sum(scalars, ids_all, recv_hidden, grads)
    return place, [back.reshape(experts * capacity, hidden_units)], weight_grad


def local(out_grad, saved_hidden, expert_ids, gate_weights, trained, down_weight):
    experts = lax.axis_size("expert")
    tokens, top_count, _ = saved_hidden.shape
    capacity = min(tokens, 3 * tokens * top_count // (2 * experts))
    hidden_t = saved_hidden.transpose(1, 0, 2)
    scalars = jnp.stack([lax.axis_index("expert").astype(I32), trained[0]])
    exchange = ring_exchange if experts == 2 * RING else gather_exchange
    place, back, weight_grad = exchange(
        out_grad, hidden_t, expert_ids.T, gate_weights.T, scalars, down_weight[0], capacity
    )
    hidden_grad, gate_grad = unpack(place.T, gate_weights, hidden_t, back)
    return hidden_grad.transpose(1, 0, 2), gate_grad.T, weight_grad[None]


def solution(mesh):
    placed = (
        P(("groups", "expert"), None),
        P(("groups", "expert"), None, None),
        P(("groups", "expert"), None),
        P(("groups", "expert"), None),
        P(("groups", "expert")),
        P("expert", None, None),
    )
    return jax.shard_map(
        local,
        mesh=mesh,
        in_specs=placed,
        out_specs=(
            P(("groups", "expert"), None, None),
            P(("groups", "expert"), None),
            P(("groups", "expert"), None, None),
        ),
        check_vma=False,
    )
```

```python
import functools

import jax
import jax.numpy as jnp
from jax import lax
from jax.experimental import pallas as pl
from jax.experimental.pallas import tpu as pltpu
from jax.sharding import PartitionSpec as P

F32, BF16, I32 = jnp.float32, jnp.bfloat16, jnp.int32
VMEM_LIMIT = 62 * 1024 * 1024


def whole(memory_space=pltpu.VMEM):
    return pl.BlockSpec(memory_space=memory_space)


def earlier(tokens):
    row = lax.broadcasted_iota(I32, (tokens, tokens), 0)
    column = lax.broadcasted_iota(I32, (tokens, tokens), 1)
    return (row < column).astype(F32).astype(BF16)


def pack_kernel(experts, capacity, ids_ref, gates_ref, hidden_ref, out_ref, place_ref, table, select):
    top_count, tokens = ids_ref.shape
    expert = lax.broadcasted_iota(I32, (experts, tokens), 0)
    named = jnp.zeros((experts, tokens), F32)
    for k in range(top_count):
        named = named + (ids_ref[k : k + 1, :] == expert).astype(F32)
    rank = jnp.dot(named.astype(BF16), earlier(tokens), preferred_element_type=F32).astype(I32)
    target = expert * capacity + rank
    for k in range(top_count):
        place_ref[k : k + 1, :] = jnp.sum(
            jnp.where(ids_ref[k : k + 1, :] == expert, target, 0), axis=0, keepdims=True
        )
        table[k * tokens : (k + 1) * tokens, :] = hidden_ref[k]
    rows = out_ref.shape[0]
    step = 128
    for first in range(0, rows, step):
        row = lax.broadcasted_iota(I32, (step, tokens), 0) + first
        for k in range(top_count):
            select[:, k * tokens : (k + 1) * tokens] = jnp.where(
                place_ref[k : k + 1, :] == row, gates_ref[k : k + 1, :].astype(F32), 0.0
            ).astype(BF16)
        out_ref[first : first + step, :] = jnp.dot(
            select[...], table[...], preferred_element_type=F32
        ).astype(BF16)


def pack(ids_t, gates_t, hidden_t, experts, capacity):
    top_count, tokens, hidden_units = hidden_t.shape
    return pl.pallas_call(
        functools.partial(pack_kernel, experts, capacity),
        out_shape=(
            jax.ShapeDtypeStruct((experts * capacity, hidden_units), BF16),
            jax.ShapeDtypeStruct((top_count, tokens), I32),
        ),
        in_specs=[whole()] * 3,
        out_specs=(whole(), whole()),
        scratch_shapes=[
            pltpu.VMEM((top_count * tokens, hidden_units), BF16),
            pltpu.VMEM((128, top_count * tokens), BF16),
        ],
        compiler_params=pltpu.CompilerParams(vmem_limit_bytes=VMEM_LIMIT),
        name="pack",
    )(ids_t, gates_t, hidden_t)


def source_rank(ids, expert, tokens):
    named = jnp.max((ids == expert).astype(F32), axis=0, keepdims=True)
    rank = jnp.dot(named.astype(BF16), earlier(tokens), preferred_element_type=F32)
    return jnp.where(named > 0.5, rank.astype(I32), -1)


def upstream_kernel(capacity, expert_ref, ids_ref, grad_ref, weight_ref, out_ref):
    tokens = grad_ref.shape[0]
    dense = lax.dot_general(
        grad_ref[...], weight_ref[...], (((1,), (1,)), ((), ())), preferred_element_type=F32
    ).astype(BF16)
    rank = source_rank(ids_ref[0], expert_ref[0], tokens)
    choose = (rank == lax.broadcasted_iota(I32, (capacity, tokens), 0)).astype(F32).astype(BF16)
    out_ref[0] = jnp.dot(choose, dense, preferred_element_type=F32).astype(BF16)


def upstream(expert, ids_all, grads, weight, capacity):
    sources, top_count, tokens = ids_all.shape
    hidden_units, width = weight.shape
    return pl.pallas_call(
        functools.partial(upstream_kernel, capacity),
        out_shape=jax.ShapeDtypeStruct((sources, capacity, hidden_units), BF16),
        grid_spec=pltpu.PrefetchScalarGridSpec(
            num_scalar_prefetch=1,
            grid=(sources,),
            in_specs=[
                pl.BlockSpec((1, top_count, tokens), lambda j, e: (j, 0, 0)),
                pl.BlockSpec((tokens, width), lambda j, e: (j, 0)),
                pl.BlockSpec((hidden_units, width), lambda j, e: (0, 0)),
            ],
            out_specs=pl.BlockSpec((1, capacity, hidden_units), lambda j, e: (j, 0, 0)),
        ),
        compiler_params=pltpu.CompilerParams(vmem_limit_bytes=VMEM_LIMIT),
        name="upstream",
    )(expert, ids_all, grads, weight)


def weight_kernel(scalar_ref, ids_ref, hidden_ref, grad_ref, out_ref, dense):
    sources, top_count, tokens = ids_ref.shape
    capacity = hidden_ref.shape[1]

    @pl.when(pl.program_id(0) == 0)
    def _():
        for j in range(sources):
            rank = source_rank(ids_ref[j], scalar_ref[0], tokens)
            choose = (rank == lax.broadcasted_iota(I32, (capacity, tokens), 0)).astype(F32).astype(BF16)
            dense[:, j * tokens : (j + 1) * tokens] = lax.dot_general(
                hidden_ref[j], choose, (((0,), (0,)), ((), ())), preferred_element_type=F32
            ).astype(BF16)

    total = jnp.dot(dense[...], grad_ref[...], preferred_element_type=F32)
    out_ref[...] = (total * scalar_ref[1].astype(F32)).astype(BF16)


def weight_sum(scalars, ids_all, recv_hidden, grads):
    sources, capacity, hidden_units = recv_hidden.shape
    _, top_count, tokens = ids_all.shape
    rows, width = grads.shape
    step = 256
    return pl.pallas_call(
        weight_kernel,
        out_shape=jax.ShapeDtypeStruct((hidden_units, width), BF16),
        grid_spec=pltpu.PrefetchScalarGridSpec(
            num_scalar_prefetch=1,
            grid=(width // step,),
            in_specs=[
                pl.BlockSpec((sources, top_count, tokens), lambda n, e: (0, 0, 0)),
                pl.BlockSpec((sources, capacity, hidden_units), lambda n, e: (0, 0, 0)),
                pl.BlockSpec((rows, step), lambda n, e: (0, n)),
            ],
            out_specs=pl.BlockSpec((hidden_units, step), lambda n, e: (0, n)),
            scratch_shapes=[pltpu.VMEM((hidden_units, rows), BF16)],
        ),
        compiler_params=pltpu.CompilerParams(vmem_limit_bytes=VMEM_LIMIT),
        name="weight_sum",
    )(scalars, ids_all, recv_hidden, grads)


RING = 8
COLUMNS = 4
COPIES = 2 * COLUMNS + 1
ADD_LIMIT = 24 * 1024 * 1024
ID_ROWS = 8
PARTS = 4
UNPACK_FLOPS = 40_000_000_000
OFFSETS = (0, -1, 1, -2, 2, -3, 3, 4)
SWAP = [(i, i ^ 1) for i in range(16)]


def ring_device(position, core):
    z, y = (position, 0) if position < 4 else (7 - position, 1)
    return (z * 2 + y) * 2 + core


def ring_shift(step):
    return [
        (ring_device(p, core), ring_device((p + step) % RING, core))
        for p in range(RING)
        for core in range(2)
    ]


def ring_position(device):
    z, y = device >> 2, (device >> 1) & 1
    return jnp.where(y == 0, z, 7 - z)


def ring_pack_kernel(capacity, me_ref, ids_ref, gates_ref, hidden_ref, *rest):
    outs, (place_ref, table, select, blocks, sems) = rest[:RING], rest[RING:]
    top_count, tokens = ids_ref.shape
    experts = 2 * RING
    expert = lax.broadcasted_iota(I32, (experts, tokens), 0)
    named = jnp.zeros((experts, tokens), F32)
    for k in range(top_count):
        named = named + (ids_ref[k : k + 1, :] == expert).astype(F32)
    rank = jnp.dot(named.astype(BF16), earlier(tokens), preferred_element_type=F32).astype(I32)
    me = me_ref[0]
    target = (ring_position(expert) * 2 + ((expert & 1) ^ (me & 1))) * capacity + rank
    for k in range(top_count):
        place_ref[k : k + 1, :] = jnp.sum(
            jnp.where(ids_ref[k : k + 1, :] == expert, target, 0), axis=0, keepdims=True
        )
        table[k * tokens : (k + 1) * tokens, :] = hidden_ref[k]
    step = 2 * capacity
    copies = []
    for d in range(RING):
        row = lax.broadcasted_iota(I32, (step, tokens), 0) + ((ring_position(me) + d) & 7) * step
        for k in range(top_count):
            select[:, k * tokens : (k + 1) * tokens] = jnp.where(
                place_ref[k : k + 1, :] == row, gates_ref[k : k + 1, :].astype(F32), 0.0
            ).astype(BF16)
        blocks[d] = jnp.dot(select[...], table[...], preferred_element_type=F32).astype(BF16)
        copies.append(pltpu.make_async_copy(blocks.at[d], outs[d], sems.at[d]))
        copies[-1].start()
    for copy in copies:
        copy.wait()


def ring_pack(me, ids_t, gates_t, hidden_t, capacity):
    top_count, tokens, hidden_units = hidden_t.shape
    block = jax.ShapeDtypeStruct((2 * capacity, hidden_units), BF16)
    *blocks, place = pl.pallas_call(
        functools.partial(ring_pack_kernel, capacity),
        out_shape=(block,) * RING + (jax.ShapeDtypeStruct((top_count, tokens), I32),),
        in_specs=[whole(pltpu.SMEM)] + [whole()] * 3,
        out_specs=(whole(pltpu.HBM),) * RING + (whole(),),
        scratch_shapes=[
            pltpu.VMEM((top_count * tokens, hidden_units), BF16),
            pltpu.VMEM((2 * capacity, top_count * tokens), BF16),
            pltpu.VMEM((RING, 2 * capacity, hidden_units), BF16),
            pltpu.SemaphoreType.DMA((RING,)),
        ],
        compiler_params=pltpu.CompilerParams(vmem_limit_bytes=VMEM_LIMIT),
        cost_estimate=pl.CostEstimate(flops=3_000_000_000, bytes_accessed=5_000_000, transcendentals=0),
        name="pack",
    )(me, ids_t, gates_t, hidden_t)
    return blocks, place


def both_ranks(ids, me, capacity, tokens):
    own = source_rank(ids, me, tokens)
    other = source_rank(ids, me ^ 1, tokens)
    return own, jnp.where(other >= 0, other + capacity, -1)


def load(refs, buffer, sems, first):
    copies, at = [], 0
    for n, ref in enumerate(refs):
        copies.append(
            pltpu.make_async_copy(ref, buffer.at[pl.ds(at, ref.shape[0])], sems.at[first + n])
        )
        copies[-1].start()
        at += ref.shape[0]
    return copies


def load_pieces(refs, grads, ids, sems, first):
    half, wide = ids.shape[2] // 2, grads.shape[1] // COLUMNS
    rows, routes, at = [], [], 0
    for ref in refs:
        extra = ref.shape[0] % 16
        for base in range(0, ref.shape[0] - extra, half * COLUMNS):
            for column in range(COLUMNS):
                rows.append(
                    pltpu.make_async_copy(
                        ref.at[pl.ds(base + column * half, half)],
                        grads.at[pl.ds(at, half), pl.ds(column * wide, wide)],
                        sems.at[first + len(rows) + len(routes)],
                    )
                )
            at += half
        if extra:
            routes.append(
                pltpu.make_async_copy(
                    ref.at[pl.ds(ref.shape[0] - extra, extra), pl.ds(0, 2 * half)],
                    ids.at[at // (2 * half) - 1],
                    sems.at[first + len(rows) + len(routes)],
                )
            )
    for copy in routes + rows:
        copy.start()
    return routes, rows


def ring_upstream_kernel(capacity, offsets, pieces, me_ref, own_ref, other_ref, *rest):
    blocks = len(offsets)
    grad_refs, (out_ref, weights, grads, ids, dense, rows, sems, out_sems) = rest[:pieces], rest[-8:]
    tokens = ids.shape[2]
    me = me_ref[0]
    routes, loads = load_pieces(grad_refs, grads, ids, sems, 2)
    loads += routes
    weight_loads = [
        pltpu.make_async_copy(own_ref, weights.at[0], sems.at[0]),
        pltpu.make_async_copy(other_ref, weights.at[1], sems.at[1]),
    ]
    for copy in weight_loads:
        copy.start()
    for copy in loads:
        copy.wait()
    for i in range(2):
        weight_loads[i].wait()
        product = lax.dot_general(
            grads[...], weights[i], (((1,), (1,)), ((), ())), preferred_element_type=F32
        ).astype(BF16)
        for b in range(blocks):
            dense[b, i * tokens : (i + 1) * tokens, :] = product[b * tokens : (b + 1) * tokens, :]
    row = lax.broadcasted_iota(I32, (2 * capacity, 2 * tokens), 0)
    copies = []
    for b, offset in enumerate(offsets):
        ranks = both_ranks(ids[b].astype(F32).astype(I32), me, capacity, tokens)
        choose = (jnp.concatenate(ranks, axis=1) == row).astype(F32).astype(BF16)
        rows[b] = jnp.dot(choose, dense[b], preferred_element_type=F32).astype(BF16)
        goal = out_ref.at[(ring_position(me) + offset + RING) & 7]
        copies.append(pltpu.make_async_copy(rows.at[b], goal, out_sems.at[b]))
        copies[-1].start()
    for copy in copies:
        copy.wait()


def ring_upstream(me, tokens, offsets, pieces, so_far, own_weight, other_weight, capacity):
    hidden_units, width = own_weight.shape
    blocks = len(offsets)
    return pl.pallas_call(
        functools.partial(ring_upstream_kernel, capacity, offsets, len(pieces)),
        out_shape=jax.ShapeDtypeStruct((RING, 2 * capacity, hidden_units), BF16),
        in_specs=[whole(pltpu.SMEM)] + [whole(pltpu.HBM)] * (2 + len(pieces) + len(so_far)),
        out_specs=whole(pltpu.HBM),
        input_output_aliases={3 + len(pieces): 0} if so_far else {},
        scratch_shapes=[
            pltpu.VMEM((2, hidden_units, width), BF16),
            pltpu.VMEM((blocks * tokens, width), BF16),
            pltpu.VMEM((blocks, ID_ROWS, tokens), BF16),
            pltpu.VMEM((blocks, 2 * tokens, hidden_units), BF16),
            pltpu.VMEM((blocks, 2 * capacity, hidden_units), BF16),
            pltpu.SemaphoreType.DMA((2 + COPIES * blocks,)),
            pltpu.SemaphoreType.DMA((blocks,)),
        ],
        compiler_params=pltpu.CompilerParams(vmem_limit_bytes=VMEM_LIMIT),
        cost_estimate=pl.CostEstimate(
            flops=4 * blocks * tokens * hidden_units * width,
            bytes_accessed=2 * (blocks * tokens + 2 * hidden_units) * width,
            transcendentals=0,
        ),
        name="upstream",
    )(me, own_weight, other_weight, *pieces, *so_far)


def ring_weight_kernel(capacity, other, pieces, me_ref, *rest):
    grad_refs, hidden_refs = rest[:pieces], rest[pieces : pieces + RING]
    outs, (grads, ids, hidden, dense, sems) = rest[pieces + RING : -5], rest[-5:]
    tokens = ids.shape[2]
    me = me_ref[0]
    routes, grad_loads = load_pieces(grad_refs, grads, ids, sems, 0)
    loads = [
        pltpu.make_async_copy(ref, hidden.at[q], sems.at[COPIES * RING + q])
        for q, ref in enumerate(hidden_refs)
    ]
    for copy in loads:
        copy.start()
    for copy in routes + loads:
        copy.wait()
    row = lax.broadcasted_iota(I32, (2 * capacity, tokens), 0)
    for q in range(RING):
        rank = both_ranks(ids[q].astype(F32).astype(I32), me, capacity, tokens)[other]
        choose = (rank == row).astype(F32).astype(BF16)
        dense[:, q * tokens : (q + 1) * tokens] = lax.dot_general(
            hidden[q], choose, (((0,), (0,)), ((), ())), preferred_element_type=F32
        ).astype(BF16)
    for copy in grad_loads:
        copy.wait()
    width = grads.shape[1]
    step = 512

    @pl.loop(0, width // step)
    def _(n):
        at = pl.ds(pl.multiple_of(n * step, step), step)
        total = jnp.dot(dense[...], grads[:, at], preferred_element_type=F32)
        height = total.shape[0] // len(outs)
        for part, part_ref in enumerate(outs):
            part_ref[:, at] = total[part * height : (part + 1) * height].astype(BF16)


def ring_weight_sum(me, tokens, pieces, hidden, other, capacity):
    width = pieces[0].shape[1] * COLUMNS
    hidden_units = hidden[0].shape[1]
    result = jax.ShapeDtypeStruct((hidden_units // PARTS, width), BF16)
    return pl.pallas_call(
        functools.partial(ring_weight_kernel, capacity, other, len(pieces)),
        out_shape=(result,) * PARTS,
        in_specs=[whole(pltpu.SMEM)] + [whole(pltpu.HBM)] * (len(pieces) + RING),
        out_specs=(whole(),) * PARTS,
        scratch_shapes=[
            pltpu.VMEM((RING * tokens, width), BF16),
            pltpu.VMEM((RING, ID_ROWS, tokens), BF16),
            pltpu.VMEM((RING, 2 * capacity, hidden_units), BF16),
            pltpu.VMEM((hidden_units, RING * tokens), BF16),
            pltpu.SemaphoreType.DMA((COPIES * RING + RING,)),
        ],
        compiler_params=pltpu.CompilerParams(vmem_limit_bytes=VMEM_LIMIT),
        cost_estimate=pl.CostEstimate(flops=1_000_000, bytes_accessed=1_000_000, transcendentals=0),
        name="weight_other" if other else "weight_own",
    )(me, *pieces, *hidden)


def add_kernel(trained_ref, *rest):
    own_refs, came_refs, (out_ref, own, came, sums, sems) = rest[:PARTS], rest[PARTS : 2 * PARTS], rest[-5:]
    trained = trained_ref[0].astype(F32)
    height = own.shape[1]
    loads = []
    for part in range(PARTS):
        for n, (ref, buffer) in enumerate(((own_refs[part], own), (came_refs[part], came))):
            loads.append(pltpu.make_async_copy(ref, buffer.at[part], sems.at[n, part]))
            loads[-1].start()
    stores = []
    for part in range(PARTS):
        loads[2 * part].wait()
        loads[2 * part + 1].wait()
        total = own[part].astype(F32) + came[part].astype(F32)
        sums[part] = (total * trained).astype(BF16)
        goal = out_ref.at[pl.ds(part * height, height)]
        stores.append(pltpu.make_async_copy(sums.at[part], goal, sems.at[2, part]))
        stores[-1].start()
    for copy in stores:
        copy.wait()


def add_parts(trained, own, came):
    height, width = own[0].shape
    return pl.pallas_call(
        add_kernel,
        out_shape=jax.ShapeDtypeStruct((height * PARTS, width), BF16),
        in_specs=[whole(pltpu.SMEM)] + [whole(pltpu.HBM)] * (2 * PARTS),
        out_specs=whole(pltpu.HBM),
        scratch_shapes=[pltpu.VMEM((PARTS, height, width), BF16)] * 3
        + [pltpu.SemaphoreType.DMA((3, PARTS))],
        compiler_params=pltpu.CompilerParams(vmem_limit_bytes=ADD_LIMIT),
        cost_estimate=pl.CostEstimate(flops=1_000_000, bytes_accessed=1_000_000, transcendentals=0),
        name="weight_add",
    )(trained, *own, *came)


def unpack_kernel(place_ref, gates_ref, hidden_ref, back_ref, grad_ref, gate_ref, select, sums):
    tokens, top_count = place_ref.shape
    rows = back_ref.shape[0]
    lane = lax.broadcasted_iota(I32, (tokens, rows), 1)
    for k in range(top_count):
        select[k * tokens : (k + 1) * tokens, :] = (
            (place_ref[:, k : k + 1] == lane).astype(F32).astype(BF16)
        )
    sums[...] = jnp.zeros_like(sums)
    up = jnp.dot(select[...], back_ref[...], preferred_element_type=F32)
    for k in range(top_count):
        mine = up[k * tokens : (k + 1) * tokens, :]
        grad_ref[k] = (gates_ref[:, k : k + 1].astype(F32) * mine).astype(BF16)
        sums[:, k : k + 1] = jnp.sum(hidden_ref[k].astype(F32) * mine, axis=1, keepdims=True)
    gate_ref[...] = sums[...].T[:top_count, :].astype(BF16)


def unpack(place, gates, hidden_t, back):
    top_count, tokens, hidden_units = hidden_t.shape
    rows = sum(block.shape[0] for block in back)
    return pl.pallas_call(
        unpack_kernel,
        out_shape=(
            jax.ShapeDtypeStruct((top_count, tokens, hidden_units), BF16),
            jax.ShapeDtypeStruct((top_count, tokens), BF16),
        ),
        in_specs=[whole()] * 3 + [whole()] * len(back),
        out_specs=(whole(), whole()),
        scratch_shapes=[
            pltpu.VMEM((top_count * tokens, rows), BF16),
            pltpu.VMEM((tokens, 128), F32),
        ],
        compiler_params=pltpu.CompilerParams(vmem_limit_bytes=24 * 1024 * 1024),
        cost_estimate=pl.CostEstimate(
            flops=UNPACK_FLOPS, bytes_accessed=6 * rows * hidden_units, transcendentals=0
        ),
        name="unpack",
    )(place, gates, hidden_t, *back)


def ring_exchange(out_grad, hidden_t, ids_t, gates_t, scalars, weight, capacity):
    def send(value, step):
        return lax.ppermute(value, "expert", ring_shift(step))

    me = scalars[:1]
    tokens, width = out_grad.shape
    half, wide = tokens // 2, width // COLUMNS
    cut = half * COLUMNS
    rows = out_grad.reshape(2, half, COLUMNS, wide).transpose(0, 2, 1, 3).reshape(2 * cut, wide)
    spare = ((0, ID_ROWS - ids_t.shape[0]), (0, wide - tokens))
    block = jnp.concatenate([rows, jnp.pad(ids_t.astype(BF16), spare, constant_values=-1)])
    packed, place = ring_pack(me, ids_t, gates_t, hidden_t, capacity)
    other_weight = lax.ppermute(weight, "expert", SWAP)
    barrier = lax.optimization_barrier
    hidden = [None] * RING

    def send_hidden(*chosen):
        for q in chosen:
            hidden[q] = send(packed[-OFFSETS[q] % RING], -OFFSETS[q] % RING)

    ahead, behind = send(block, 1), send(block, -1)
    ahead, behind, *packed = barrier((ahead, behind, *packed))
    pieces = [block, ahead, behind]
    hidden[0] = packed[0]
    ahead, behind = send(ahead, 1), send(behind, -1)
    ahead, behind, other_weight = barrier((ahead, behind, other_weight))
    pieces += [ahead, behind]
    upstream_of = functools.partial(
        ring_upstream, me, tokens, own_weight=weight, other_weight=other_weight, capacity=capacity
    )
    ahead, behind = send(ahead, 1), send(behind, -1)
    send_hidden(3, 4)
    up = upstream_of(OFFSETS[:5], pieces[:5], ())
    pieces += [ahead, behind]
    ahead, behind, hidden[3], hidden[4], up = barrier(
        (ahead[:cut], behind[cut:], hidden[3], hidden[4], up)
    )
    pieces += [send(ahead, 1), send(behind, -1)]
    send_hidden(5, 6, 7, 1, 2)
    up = upstream_of(OFFSETS[5:], pieces[5:], (up,))
    *hidden, up = barrier((*hidden, up))
    groups = [[ring_device(p, core) for p in range(RING)] for core in range(2)]
    back = lax.all_to_all(up, "expert", 0, 0, axis_index_groups=groups, tiled=True)
    theirs = ring_weight_sum(me, tokens, pieces, hidden, True, capacity)
    came = [lax.ppermute(part, "expert", SWAP) for part in theirs]
    own = ring_weight_sum(me, tokens, pieces, hidden, False, capacity)
    weight_grad = add_parts(scalars[1:], own, came)
    place, weight_grad = barrier((place, weight_grad))
    return place, [back.reshape(-1, back.shape[2])], weight_grad


def gather_exchange(out_grad, hidden_t, ids_t, gates_t, scalars, weight, capacity):
    experts = lax.axis_size("expert")
    hidden_units = weight.shape[0]
    ids_all = lax.all_gather(ids_t, "expert", axis=0)
    packed, place = pack(ids_t, gates_t, hidden_t, experts, capacity)
    grads = lax.all_gather(out_grad, "expert", axis=0, tiled=True)
    recv_hidden = lax.all_to_all(
        packed.reshape(experts, capacity, hidden_units), "expert", 0, 0, tiled=True
    )
    up = upstream(scalars[:1], ids_all, grads, weight, capacity)
    back = lax.all_to_all(up, "expert", 0, 0, tiled=True)
    weight_grad = weight_sum(scalars, ids_all, recv_hidden, grads)
    return place, [back.reshape(experts * capacity, hidden_units)], weight_grad


def local(out_grad, saved_hidden, expert_ids, gate_weights, trained, down_weight):
    experts = lax.axis_size("expert")
    tokens, top_count, _ = saved_hidden.shape
    capacity = min(tokens, 3 * tokens * top_count // (2 * experts))
    hidden_t = saved_hidden.transpose(1, 0, 2)
    scalars = jnp.stack([lax.axis_index("expert").astype(I32), trained[0]])
    exchange = ring_exchange if experts == 2 * RING else gather_exchange
    place, back, weight_grad = exchange(
        out_grad, hidden_t, expert_ids.T, gate_weights.T, scalars, down_weight[0], capacity
    )
    hidden_grad, gate_grad = unpack(place.T, gate_weights, hidden_t, back)
    return hidden_grad.transpose(1, 0, 2), gate_grad.T, weight_grad[None]


def solution(mesh):
    placed = (
        P(("groups", "expert"), None),
        P(("groups", "expert"), None, None),
        P(("groups", "expert"), None),
        P(("groups", "expert"), None),
        P(("groups", "expert")),
        P("expert", None, None),
    )
    return jax.shard_map(
        local,
        mesh=mesh,
        in_specs=placed,
        out_specs=(
            P(("groups", "expert"), None, None),
            P(("groups", "expert"), None),
            P(("groups", "expert"), None, None),
        ),
        check_vma=False,
    )
```

```python
import functools

import jax
import jax.numpy as jnp
from jax import lax
from jax.experimental import pallas as pl
from jax.experimental.pallas import tpu as pltpu
from jax.sharding import PartitionSpec as P

F32, BF16, I32 = jnp.float32, jnp.bfloat16, jnp.int32
VMEM_LIMIT = 62 * 1024 * 1024


def whole(memory_space=pltpu.VMEM):
    return pl.BlockSpec(memory_space=memory_space)


def earlier(tokens):
    row = lax.broadcasted_iota(I32, (tokens, tokens), 0)
    column = lax.broadcasted_iota(I32, (tokens, tokens), 1)
    return (row < column).astype(F32).astype(BF16)


def pack_kernel(experts, capacity, ids_ref, gates_ref, hidden_ref, out_ref, place_ref, table, select):
    top_count, tokens = ids_ref.shape
    expert = lax.broadcasted_iota(I32, (experts, tokens), 0)
    named = jnp.zeros((experts, tokens), F32)
    for k in range(top_count):
        named = named + (ids_ref[k : k + 1, :] == expert).astype(F32)
    rank = jnp.dot(named.astype(BF16), earlier(tokens), preferred_element_type=F32).astype(I32)
    target = expert * capacity + rank
    for k in range(top_count):
        place_ref[k : k + 1, :] = jnp.sum(
            jnp.where(ids_ref[k : k + 1, :] == expert, target, 0), axis=0, keepdims=True
        )
        table[k * tokens : (k + 1) * tokens, :] = hidden_ref[k]
    rows = out_ref.shape[0]
    step = 128
    for first in range(0, rows, step):
        row = lax.broadcasted_iota(I32, (step, tokens), 0) + first
        for k in range(top_count):
            select[:, k * tokens : (k + 1) * tokens] = jnp.where(
                place_ref[k : k + 1, :] == row, gates_ref[k : k + 1, :].astype(F32), 0.0
            ).astype(BF16)
        out_ref[first : first + step, :] = jnp.dot(
            select[...], table[...], preferred_element_type=F32
        ).astype(BF16)


def pack(ids_t, gates_t, hidden_t, experts, capacity):
    top_count, tokens, hidden_units = hidden_t.shape
    return pl.pallas_call(
        functools.partial(pack_kernel, experts, capacity),
        out_shape=(
            jax.ShapeDtypeStruct((experts * capacity, hidden_units), BF16),
            jax.ShapeDtypeStruct((top_count, tokens), I32),
        ),
        in_specs=[whole()] * 3,
        out_specs=(whole(), whole()),
        scratch_shapes=[
            pltpu.VMEM((top_count * tokens, hidden_units), BF16),
            pltpu.VMEM((128, top_count * tokens), BF16),
        ],
        compiler_params=pltpu.CompilerParams(vmem_limit_bytes=VMEM_LIMIT),
        name="pack",
    )(ids_t, gates_t, hidden_t)


def source_rank(ids, expert, tokens):
    named = jnp.max((ids == expert).astype(F32), axis=0, keepdims=True)
    rank = jnp.dot(named.astype(BF16), earlier(tokens), preferred_element_type=F32)
    return jnp.where(named > 0.5, rank.astype(I32), -1)


def upstream_kernel(capacity, expert_ref, ids_ref, grad_ref, weight_ref, out_ref):
    tokens = grad_ref.shape[0]
    dense = lax.dot_general(
        grad_ref[...], weight_ref[...], (((1,), (1,)), ((), ())), preferred_element_type=F32
    ).astype(BF16)
    rank = source_rank(ids_ref[0], expert_ref[0], tokens)
    choose = (rank == lax.broadcasted_iota(I32, (capacity, tokens), 0)).astype(F32).astype(BF16)
    out_ref[0] = jnp.dot(choose, dense, preferred_element_type=F32).astype(BF16)


def upstream(expert, ids_all, grads, weight, capacity):
    sources, top_count, tokens = ids_all.shape
    hidden_units, width = weight.shape
    return pl.pallas_call(
        functools.partial(upstream_kernel, capacity),
        out_shape=jax.ShapeDtypeStruct((sources, capacity, hidden_units), BF16),
        grid_spec=pltpu.PrefetchScalarGridSpec(
            num_scalar_prefetch=1,
            grid=(sources,),
            in_specs=[
                pl.BlockSpec((1, top_count, tokens), lambda j, e: (j, 0, 0)),
                pl.BlockSpec((tokens, width), lambda j, e: (j, 0)),
                pl.BlockSpec((hidden_units, width), lambda j, e: (0, 0)),
            ],
            out_specs=pl.BlockSpec((1, capacity, hidden_units), lambda j, e: (j, 0, 0)),
        ),
        compiler_params=pltpu.CompilerParams(vmem_limit_bytes=VMEM_LIMIT),
        name="upstream",
    )(expert, ids_all, grads, weight)


def weight_kernel(scalar_ref, ids_ref, hidden_ref, grad_ref, out_ref, dense):
    sources, top_count, tokens = ids_ref.shape
    capacity = hidden_ref.shape[1]

    @pl.when(pl.program_id(0) == 0)
    def _():
        for j in range(sources):
            rank = source_rank(ids_ref[j], scalar_ref[0], tokens)
            choose = (rank == lax.broadcasted_iota(I32, (capacity, tokens), 0)).astype(F32).astype(BF16)
            dense[:, j * tokens : (j + 1) * tokens] = lax.dot_general(
                hidden_ref[j], choose, (((0,), (0,)), ((), ())), preferred_element_type=F32
            ).astype(BF16)

    total = jnp.dot(dense[...], grad_ref[...], preferred_element_type=F32)
    out_ref[...] = (total * scalar_ref[1].astype(F32)).astype(BF16)


def weight_sum(scalars, ids_all, recv_hidden, grads):
    sources, capacity, hidden_units = recv_hidden.shape
    _, top_count, tokens = ids_all.shape
    rows, width = grads.shape
    step = 256
    return pl.pallas_call(
        weight_kernel,
        out_shape=jax.ShapeDtypeStruct((hidden_units, width), BF16),
        grid_spec=pltpu.PrefetchScalarGridSpec(
            num_scalar_prefetch=1,
            grid=(width // step,),
            in_specs=[
                pl.BlockSpec((sources, top_count, tokens), lambda n, e: (0, 0, 0)),
                pl.BlockSpec((sources, capacity, hidden_units), lambda n, e: (0, 0, 0)),
                pl.BlockSpec((rows, step), lambda n, e: (0, n)),
            ],
            out_specs=pl.BlockSpec((hidden_units, step), lambda n, e: (0, n)),
            scratch_shapes=[pltpu.VMEM((hidden_units, rows), BF16)],
        ),
        compiler_params=pltpu.CompilerParams(vmem_limit_bytes=VMEM_LIMIT),
        name="weight_sum",
    )(scalars, ids_all, recv_hidden, grads)


RING = 8
COLUMNS = 4
COPIES = 2 * COLUMNS + 1
ADD_LIMIT = 24 * 1024 * 1024
ID_ROWS = 8
PARTS = 4
UNPACK_FLOPS = 40_000_000_000
OFFSETS = (0, -1, 1, -2, 2, -3, 3, 4)
SWAP = [(i, i ^ 1) for i in range(16)]


def ring_device(position, core):
    z, y = (position, 0) if position < 4 else (7 - position, 1)
    return (z * 2 + y) * 2 + core


def ring_shift(step):
    return [
        (ring_device(p, core), ring_device((p + step) % RING, core))
        for p in range(RING)
        for core in range(2)
    ]


def ring_position(device):
    z, y = device >> 2, (device >> 1) & 1
    return jnp.where(y == 0, z, 7 - z)


def ring_pack_kernel(capacity, me_ref, ids_ref, gates_ref, hidden_ref, *rest):
    outs, (place_ref, table, select, blocks, sems) = rest[:RING], rest[RING:]
    top_count, tokens = ids_ref.shape
    experts = 2 * RING
    expert = lax.broadcasted_iota(I32, (experts, tokens), 0)
    named = jnp.zeros((experts, tokens), F32)
    for k in range(top_count):
        named = named + (ids_ref[k : k + 1, :] == expert).astype(F32)
    rank = jnp.dot(named.astype(BF16), earlier(tokens), preferred_element_type=F32).astype(I32)
    me = me_ref[0]
    target = (ring_position(expert) * 2 + ((expert & 1) ^ (me & 1))) * capacity + rank
    for k in range(top_count):
        place_ref[k : k + 1, :] = jnp.sum(
            jnp.where(ids_ref[k : k + 1, :] == expert, target, 0), axis=0, keepdims=True
        )
        table[k * tokens : (k + 1) * tokens, :] = hidden_ref[k]
    step = 2 * capacity
    copies = []
    for d in range(RING):
        row = lax.broadcasted_iota(I32, (step, tokens), 0) + ((ring_position(me) + d) & 7) * step
        for k in range(top_count):
            select[:, k * tokens : (k + 1) * tokens] = jnp.where(
                place_ref[k : k + 1, :] == row, gates_ref[k : k + 1, :].astype(F32), 0.0
            ).astype(BF16)
        blocks[d] = jnp.dot(select[...], table[...], preferred_element_type=F32).astype(BF16)
        copies.append(pltpu.make_async_copy(blocks.at[d], outs[d], sems.at[d]))
        copies[-1].start()
    for copy in copies:
        copy.wait()


def ring_pack(me, ids_t, gates_t, hidden_t, capacity):
    top_count, tokens, hidden_units = hidden_t.shape
    block = jax.ShapeDtypeStruct((2 * capacity, hidden_units), BF16)
    *blocks, place = pl.pallas_call(
        functools.partial(ring_pack_kernel, capacity),
        out_shape=(block,) * RING + (jax.ShapeDtypeStruct((top_count, tokens), I32),),
        in_specs=[whole(pltpu.SMEM)] + [whole()] * 3,
        out_specs=(whole(pltpu.HBM),) * RING + (whole(),),
        scratch_shapes=[
            pltpu.VMEM((top_count * tokens, hidden_units), BF16),
            pltpu.VMEM((2 * capacity, top_count * tokens), BF16),
            pltpu.VMEM((RING, 2 * capacity, hidden_units), BF16),
            pltpu.SemaphoreType.DMA((RING,)),
        ],
        compiler_params=pltpu.CompilerParams(vmem_limit_bytes=VMEM_LIMIT),
        cost_estimate=pl.CostEstimate(flops=3_000_000_000, bytes_accessed=5_000_000, transcendentals=0),
        name="pack",
    )(me, ids_t, gates_t, hidden_t)
    return blocks, place


def both_ranks(ids, me, capacity, tokens):
    own = source_rank(ids, me, tokens)
    other = source_rank(ids, me ^ 1, tokens)
    return own, jnp.where(other >= 0, other + capacity, -1)


def load(refs, buffer, sems, first):
    copies, at = [], 0
    for n, ref in enumerate(refs):
        copies.append(
            pltpu.make_async_copy(ref, buffer.at[pl.ds(at, ref.shape[0])], sems.at[first + n])
        )
        copies[-1].start()
        at += ref.shape[0]
    return copies


def load_pieces(refs, grads, ids, sems, first):
    half, wide = ids.shape[2] // 2, grads.shape[1] // COLUMNS
    rows, routes, at = [], [], 0
    for ref in refs:
        extra = ref.shape[0] % 16
        for base in range(0, ref.shape[0] - extra, half * COLUMNS):
            for column in range(COLUMNS):
                rows.append(
                    pltpu.make_async_copy(
                        ref.at[pl.ds(base + column * half, half)],
                        grads.at[pl.ds(at, half), pl.ds(column * wide, wide)],
                        sems.at[first + len(rows) + len(routes)],
                    )
                )
            at += half
        if extra:
            routes.append(
                pltpu.make_async_copy(
                    ref.at[pl.ds(ref.shape[0] - extra, extra), pl.ds(0, 2 * half)],
                    ids.at[at // (2 * half) - 1],
                    sems.at[first + len(rows) + len(routes)],
                )
            )
    for copy in routes + rows:
        copy.start()
    return routes, rows


def ring_upstream_kernel(capacity, offsets, pieces, me_ref, own_ref, other_ref, *rest):
    blocks = len(offsets)
    grad_refs, (out_ref, weights, grads, ids, dense, rows, sems, out_sems) = rest[:pieces], rest[-8:]
    tokens = ids.shape[2]
    me = me_ref[0]
    routes, loads = load_pieces(grad_refs, grads, ids, sems, 2)
    loads += routes
    weight_loads = [
        pltpu.make_async_copy(own_ref, weights.at[0], sems.at[0]),
        pltpu.make_async_copy(other_ref, weights.at[1], sems.at[1]),
    ]
    for copy in weight_loads:
        copy.start()
    for copy in loads:
        copy.wait()
    for i in range(2):
        weight_loads[i].wait()
        product = lax.dot_general(
            grads[...], weights[i], (((1,), (1,)), ((), ())), preferred_element_type=F32
        ).astype(BF16)
        for b in range(blocks):
            dense[b, i * tokens : (i + 1) * tokens, :] = product[b * tokens : (b + 1) * tokens, :]
    row = lax.broadcasted_iota(I32, (2 * capacity, 2 * tokens), 0)
    copies = []
    for b, offset in enumerate(offsets):
        ranks = both_ranks(ids[b].astype(F32).astype(I32), me, capacity, tokens)
        choose = (jnp.concatenate(ranks, axis=1) == row).astype(F32).astype(BF16)
        rows[b] = jnp.dot(choose, dense[b], preferred_element_type=F32).astype(BF16)
        goal = out_ref.at[(ring_position(me) + offset + RING) & 7]
        copies.append(pltpu.make_async_copy(rows.at[b], goal, out_sems.at[b]))
        copies[-1].start()
    for copy in copies:
        copy.wait()


def ring_upstream(me, tokens, offsets, pieces, so_far, own_weight, other_weight, capacity):
    hidden_units, width = own_weight.shape
    blocks = len(offsets)
    return pl.pallas_call(
        functools.partial(ring_upstream_kernel, capacity, offsets, len(pieces)),
        out_shape=jax.ShapeDtypeStruct((RING, 2 * capacity, hidden_units), BF16),
        in_specs=[whole(pltpu.SMEM)] + [whole(pltpu.HBM)] * (2 + len(pieces) + len(so_far)),
        out_specs=whole(pltpu.HBM),
        input_output_aliases={3 + len(pieces): 0} if so_far else {},
        scratch_shapes=[
            pltpu.VMEM((2, hidden_units, width), BF16),
            pltpu.VMEM((blocks * tokens, width), BF16),
            pltpu.VMEM((blocks, ID_ROWS, tokens), BF16),
            pltpu.VMEM((blocks, 2 * tokens, hidden_units), BF16),
            pltpu.VMEM((blocks, 2 * capacity, hidden_units), BF16),
            pltpu.SemaphoreType.DMA((2 + COPIES * blocks,)),
            pltpu.SemaphoreType.DMA((blocks,)),
        ],
        compiler_params=pltpu.CompilerParams(vmem_limit_bytes=VMEM_LIMIT),
        cost_estimate=pl.CostEstimate(
            flops=4 * blocks * tokens * hidden_units * width,
            bytes_accessed=2 * (blocks * tokens + 2 * hidden_units) * width,
            transcendentals=0,
        ),
        name="upstream",
    )(me, own_weight, other_weight, *pieces, *so_far)


def ring_weight_kernel(capacity, other, pieces, me_ref, *rest):
    grad_refs, hidden_refs = rest[:pieces], rest[pieces : pieces + RING]
    outs, (grads, ids, hidden, dense, sems) = rest[pieces + RING : -5], rest[-5:]
    tokens = ids.shape[2]
    me = me_ref[0]
    routes, grad_loads = load_pieces(grad_refs, grads, ids, sems, 0)
    loads = [
        pltpu.make_async_copy(ref, hidden.at[q], sems.at[COPIES * RING + q])
        for q, ref in enumerate(hidden_refs)
    ]
    for copy in loads:
        copy.start()
    for copy in routes + loads:
        copy.wait()
    row = lax.broadcasted_iota(I32, (2 * capacity, tokens), 0)
    for q in range(RING):
        rank = both_ranks(ids[q].astype(F32).astype(I32), me, capacity, tokens)[other]
        choose = (rank == row).astype(F32).astype(BF16)
        dense[:, q * tokens : (q + 1) * tokens] = lax.dot_general(
            hidden[q], choose, (((0,), (0,)), ((), ())), preferred_element_type=F32
        ).astype(BF16)
    for copy in grad_loads:
        copy.wait()
    width = grads.shape[1]
    step = 512

    @pl.loop(0, width // step)
    def _(n):
        at = pl.ds(pl.multiple_of(n * step, step), step)
        total = jnp.dot(dense[...], grads[:, at], preferred_element_type=F32)
        height = total.shape[0] // len(outs)
        for part, part_ref in enumerate(outs):
            part_ref[:, at] = total[part * height : (part + 1) * height].astype(BF16)


def ring_weight_sum(me, tokens, pieces, hidden, other, capacity):
    width = pieces[0].shape[1] * COLUMNS
    hidden_units = hidden[0].shape[1]
    result = jax.ShapeDtypeStruct((hidden_units // PARTS, width), BF16)
    return pl.pallas_call(
        functools.partial(ring_weight_kernel, capacity, other, len(pieces)),
        out_shape=(result,) * PARTS,
        in_specs=[whole(pltpu.SMEM)] + [whole(pltpu.HBM)] * (len(pieces) + RING),
        out_specs=(whole(),) * PARTS,
        scratch_shapes=[
            pltpu.VMEM((RING * tokens, width), BF16),
            pltpu.VMEM((RING, ID_ROWS, tokens), BF16),
            pltpu.VMEM((RING, 2 * capacity, hidden_units), BF16),
            pltpu.VMEM((hidden_units, RING * tokens), BF16),
            pltpu.SemaphoreType.DMA((COPIES * RING + RING,)),
        ],
        compiler_params=pltpu.CompilerParams(vmem_limit_bytes=VMEM_LIMIT),
        cost_estimate=pl.CostEstimate(flops=1_000_000, bytes_accessed=1_000_000, transcendentals=0),
        name="weight_other" if other else "weight_own",
    )(me, *pieces, *hidden)


def add_kernel(trained_ref, *rest):
    own_refs, came_refs, (out_ref, own, came, sums, sems) = rest[:PARTS], rest[PARTS : 2 * PARTS], rest[-5:]
    trained = trained_ref[0].astype(F32)
    height = own.shape[1]
    loads = []
    for part in range(PARTS):
        for n, (ref, buffer) in enumerate(((own_refs[part], own), (came_refs[part], came))):
            loads.append(pltpu.make_async_copy(ref, buffer.at[part], sems.at[n, part]))
            loads[-1].start()
    stores = []
    for part in range(PARTS):
        loads[2 * part].wait()
        loads[2 * part + 1].wait()
        total = own[part].astype(F32) + came[part].astype(F32)
        sums[part] = (total * trained).astype(BF16)
        goal = out_ref.at[pl.ds(part * height, height)]
        stores.append(pltpu.make_async_copy(sums.at[part], goal, sems.at[2, part]))
        stores[-1].start()
    for copy in stores:
        copy.wait()


def add_parts(trained, own, came):
    height, width = own[0].shape
    return pl.pallas_call(
        add_kernel,
        out_shape=jax.ShapeDtypeStruct((height * PARTS, width), BF16),
        in_specs=[whole(pltpu.SMEM)] + [whole(pltpu.HBM)] * (2 * PARTS),
        out_specs=whole(pltpu.HBM),
        scratch_shapes=[pltpu.VMEM((PARTS, height, width), BF16)] * 3
        + [pltpu.SemaphoreType.DMA((3, PARTS))],
        compiler_params=pltpu.CompilerParams(vmem_limit_bytes=ADD_LIMIT),
        cost_estimate=pl.CostEstimate(flops=1_000_000, bytes_accessed=1_000_000, transcendentals=0),
        name="weight_add",
    )(trained, *own, *came)


def unpack_kernel(place_ref, gates_ref, hidden_ref, back_ref, grad_ref, gate_ref, select, sums):
    tokens, top_count = place_ref.shape
    rows = back_ref.shape[0]
    lane = lax.broadcasted_iota(I32, (tokens, rows), 1)
    for k in range(top_count):
        select[k * tokens : (k + 1) * tokens, :] = (
            (place_ref[:, k : k + 1] == lane).astype(F32).astype(BF16)
        )
    sums[...] = jnp.zeros_like(sums)
    up = jnp.dot(select[...], back_ref[...], preferred_element_type=F32)
    for k in range(top_count):
        mine = up[k * tokens : (k + 1) * tokens, :]
        grad_ref[k] = (gates_ref[:, k : k + 1].astype(F32) * mine).astype(BF16)
        sums[:, k : k + 1] = jnp.sum(hidden_ref[k].astype(F32) * mine, axis=1, keepdims=True)
    gate_ref[...] = sums[...].T[:top_count, :].astype(BF16)


def unpack(place, gates, hidden_t, back):
    top_count, tokens, hidden_units = hidden_t.shape
    rows = sum(block.shape[0] for block in back)
    return pl.pallas_call(
        unpack_kernel,
        out_shape=(
            jax.ShapeDtypeStruct((top_count, tokens, hidden_units), BF16),
            jax.ShapeDtypeStruct((top_count, tokens), BF16),
        ),
        in_specs=[whole()] * 3 + [whole()] * len(back),
        out_specs=(whole(), whole()),
        scratch_shapes=[
            pltpu.VMEM((top_count * tokens, rows), BF16),
            pltpu.VMEM((tokens, 128), F32),
        ],
        compiler_params=pltpu.CompilerParams(vmem_limit_bytes=24 * 1024 * 1024),
        cost_estimate=pl.CostEstimate(
            flops=UNPACK_FLOPS, bytes_accessed=6 * rows * hidden_units, transcendentals=0
        ),
        name="unpack",
    )(place, gates, hidden_t, *back)


def ring_exchange(out_grad, hidden_t, ids_t, gates_t, scalars, weight, capacity):
    def send(value, step):
        return lax.ppermute(value, "expert", ring_shift(step))

    me = scalars[:1]
    tokens, width = out_grad.shape
    half, wide = tokens // 2, width // COLUMNS
    cut = half * COLUMNS
    rows = out_grad.reshape(2, half, COLUMNS, wide).transpose(0, 2, 1, 3).reshape(2 * cut, wide)
    spare = ((0, ID_ROWS - ids_t.shape[0]), (0, wide - tokens))
    block = jnp.concatenate([rows, jnp.pad(ids_t.astype(BF16), spare, constant_values=-1)])
    packed, place = ring_pack(me, ids_t, gates_t, hidden_t, capacity)
    other_weight = lax.ppermute(weight, "expert", SWAP)
    barrier = lax.optimization_barrier
    hidden = [None] * RING

    def send_hidden(*chosen):
        for q in chosen:
            hidden[q] = send(packed[-OFFSETS[q] % RING], -OFFSETS[q] % RING)

    ahead, behind = send(block, 1), send(block, -1)
    ahead, behind, *packed = barrier((ahead, behind, *packed))
    pieces = [block, ahead, behind]
    hidden[0] = packed[0]
    ahead, behind = send(ahead, 1), send(behind, -1)
    ahead, behind, other_weight = barrier((ahead, behind, other_weight))
    pieces += [ahead, behind]
    upstream_of = functools.partial(
        ring_upstream, me, tokens, own_weight=weight, other_weight=other_weight, capacity=capacity
    )
    ahead, behind = send(ahead, 1), send(behind, -1)
    send_hidden(1, 2)
    up = upstream_of(OFFSETS[:5], pieces[:5], ())
    pieces += [ahead, behind]
    ahead, behind, hidden[1], hidden[2], up = barrier(
        (ahead[:cut], behind[cut:], hidden[1], hidden[2], up)
    )
    pieces += [send(ahead, 1), send(behind, -1)]
    send_hidden(5, 6, 7, 3, 4)
    up = upstream_of(OFFSETS[5:], pieces[5:], (up,))
    *hidden, up = barrier((*hidden, up))
    groups = [[ring_device(p, core) for p in range(RING)] for core in range(2)]
    back = lax.all_to_all(up, "expert", 0, 0, axis_index_groups=groups, tiled=True)
    theirs = ring_weight_sum(me, tokens, pieces, hidden, True, capacity)
    came = [lax.ppermute(part, "expert", SWAP) for part in theirs]
    own = ring_weight_sum(me, tokens, pieces, hidden, False, capacity)
    weight_grad = add_parts(scalars[1:], own, came)
    place, weight_grad = barrier((place, weight_grad))
    return place, [back.reshape(-1, back.shape[2])], weight_grad


def gather_exchange(out_grad, hidden_t, ids_t, gates_t, scalars, weight, capacity):
    experts = lax.axis_size("expert")
    hidden_units = weight.shape[0]
    ids_all = lax.all_gather(ids_t, "expert", axis=0)
    packed, place = pack(ids_t, gates_t, hidden_t, experts, capacity)
    grads = lax.all_gather(out_grad, "expert", axis=0, tiled=True)
    recv_hidden = lax.all_to_all(
        packed.reshape(experts, capacity, hidden_units), "expert", 0, 0, tiled=True
    )
    up = upstream(scalars[:1], ids_all, grads, weight, capacity)
    back = lax.all_to_all(up, "expert", 0, 0, tiled=True)
    weight_grad = weight_sum(scalars, ids_all, recv_hidden, grads)
    return place, [back.reshape(experts * capacity, hidden_units)], weight_grad


def local(out_grad, saved_hidden, expert_ids, gate_weights, trained, down_weight):
    experts = lax.axis_size("expert")
    tokens, top_count, _ = saved_hidden.shape
    capacity = min(tokens, 3 * tokens * top_count // (2 * experts))
    hidden_t = saved_hidden.transpose(1, 0, 2)
    scalars = jnp.stack([lax.axis_index("expert").astype(I32), trained[0]])
    exchange = ring_exchange if experts == 2 * RING else gather_exchange
    place, back, weight_grad = exchange(
        out_grad, hidden_t, expert_ids.T, gate_weights.T, scalars, down_weight[0], capacity
    )
    hidden_grad, gate_grad = unpack(place.T, gate_weights, hidden_t, back)
    return hidden_grad.transpose(1, 0, 2), gate_grad.T, weight_grad[None]


def solution(mesh):
    placed = (
        P(("groups", "expert"), None),
        P(("groups", "expert"), None, None),
        P(("groups", "expert"), None),
        P(("groups", "expert"), None),
        P(("groups", "expert")),
        P("expert", None, None),
    )
    return jax.shard_map(
        local,
        mesh=mesh,
        in_specs=placed,
        out_specs=(
            P(("groups", "expert"), None, None),
            P(("groups", "expert"), None),
            P(("groups", "expert"), None, None),
        ),
        check_vma=False,
    )
```

```python
import functools

import jax
import jax.numpy as jnp
from jax import lax
from jax.experimental import pallas as pl
from jax.experimental.pallas import tpu as pltpu
from jax.sharding import PartitionSpec as P

F32, BF16, I32 = jnp.float32, jnp.bfloat16, jnp.int32
VMEM_LIMIT = 62 * 1024 * 1024


def whole(memory_space=pltpu.VMEM):
    return pl.BlockSpec(memory_space=memory_space)


def earlier(tokens):
    row = lax.broadcasted_iota(I32, (tokens, tokens), 0)
    column = lax.broadcasted_iota(I32, (tokens, tokens), 1)
    return (row < column).astype(F32).astype(BF16)


def pack_kernel(experts, capacity, ids_ref, gates_ref, hidden_ref, out_ref, place_ref, table, select):
    top_count, tokens = ids_ref.shape
    expert = lax.broadcasted_iota(I32, (experts, tokens), 0)
    named = jnp.zeros((experts, tokens), F32)
    for k in range(top_count):
        named = named + (ids_ref[k : k + 1, :] == expert).astype(F32)
    rank = jnp.dot(named.astype(BF16), earlier(tokens), preferred_element_type=F32).astype(I32)
    target = expert * capacity + rank
    for k in range(top_count):
        place_ref[k : k + 1, :] = jnp.sum(
            jnp.where(ids_ref[k : k + 1, :] == expert, target, 0), axis=0, keepdims=True
        )
        table[k * tokens : (k + 1) * tokens, :] = hidden_ref[k]
    rows = out_ref.shape[0]
    step = 128
    for first in range(0, rows, step):
        row = lax.broadcasted_iota(I32, (step, tokens), 0) + first
        for k in range(top_count):
            select[:, k * tokens : (k + 1) * tokens] = jnp.where(
                place_ref[k : k + 1, :] == row, gates_ref[k : k + 1, :].astype(F32), 0.0
            ).astype(BF16)
        out_ref[first : first + step, :] = jnp.dot(
            select[...], table[...], preferred_element_type=F32
        ).astype(BF16)


def pack(ids_t, gates_t, hidden_t, experts, capacity):
    top_count, tokens, hidden_units = hidden_t.shape
    return pl.pallas_call(
        functools.partial(pack_kernel, experts, capacity),
        out_shape=(
            jax.ShapeDtypeStruct((experts * capacity, hidden_units), BF16),
            jax.ShapeDtypeStruct((top_count, tokens), I32),
        ),
        in_specs=[whole()] * 3,
        out_specs=(whole(), whole()),
        scratch_shapes=[
            pltpu.VMEM((top_count * tokens, hidden_units), BF16),
            pltpu.VMEM((128, top_count * tokens), BF16),
        ],
        compiler_params=pltpu.CompilerParams(vmem_limit_bytes=VMEM_LIMIT),
        name="pack",
    )(ids_t, gates_t, hidden_t)


def source_rank(ids, expert, tokens):
    named = jnp.max((ids == expert).astype(F32), axis=0, keepdims=True)
    rank = jnp.dot(named.astype(BF16), earlier(tokens), preferred_element_type=F32)
    return jnp.where(named > 0.5, rank.astype(I32), -1)


def upstream_kernel(capacity, expert_ref, ids_ref, grad_ref, weight_ref, out_ref):
    tokens = grad_ref.shape[0]
    dense = lax.dot_general(
        grad_ref[...], weight_ref[...], (((1,), (1,)), ((), ())), preferred_element_type=F32
    ).astype(BF16)
    rank = source_rank(ids_ref[0], expert_ref[0], tokens)
    choose = (rank == lax.broadcasted_iota(I32, (capacity, tokens), 0)).astype(F32).astype(BF16)
    out_ref[0] = jnp.dot(choose, dense, preferred_element_type=F32).astype(BF16)


def upstream(expert, ids_all, grads, weight, capacity):
    sources, top_count, tokens = ids_all.shape
    hidden_units, width = weight.shape
    return pl.pallas_call(
        functools.partial(upstream_kernel, capacity),
        out_shape=jax.ShapeDtypeStruct((sources, capacity, hidden_units), BF16),
        grid_spec=pltpu.PrefetchScalarGridSpec(
            num_scalar_prefetch=1,
            grid=(sources,),
            in_specs=[
                pl.BlockSpec((1, top_count, tokens), lambda j, e: (j, 0, 0)),
                pl.BlockSpec((tokens, width), lambda j, e: (j, 0)),
                pl.BlockSpec((hidden_units, width), lambda j, e: (0, 0)),
            ],
            out_specs=pl.BlockSpec((1, capacity, hidden_units), lambda j, e: (j, 0, 0)),
        ),
        compiler_params=pltpu.CompilerParams(vmem_limit_bytes=VMEM_LIMIT),
        name="upstream",
    )(expert, ids_all, grads, weight)


def weight_kernel(scalar_ref, ids_ref, hidden_ref, grad_ref, out_ref, dense):
    sources, top_count, tokens = ids_ref.shape
    capacity = hidden_ref.shape[1]

    @pl.when(pl.program_id(0) == 0)
    def _():
        for j in range(sources):
            rank = source_rank(ids_ref[j], scalar_ref[0], tokens)
            choose = (rank == lax.broadcasted_iota(I32, (capacity, tokens), 0)).astype(F32).astype(BF16)
            dense[:, j * tokens : (j + 1) * tokens] = lax.dot_general(
                hidden_ref[j], choose, (((0,), (0,)), ((), ())), preferred_element_type=F32
            ).astype(BF16)

    total = jnp.dot(dense[...], grad_ref[...], preferred_element_type=F32)
    out_ref[...] = (total * scalar_ref[1].astype(F32)).astype(BF16)


def weight_sum(scalars, ids_all, recv_hidden, grads):
    sources, capacity, hidden_units = recv_hidden.shape
    _, top_count, tokens = ids_all.shape
    rows, width = grads.shape
    step = 256
    return pl.pallas_call(
        weight_kernel,
        out_shape=jax.ShapeDtypeStruct((hidden_units, width), BF16),
        grid_spec=pltpu.PrefetchScalarGridSpec(
            num_scalar_prefetch=1,
            grid=(width // step,),
            in_specs=[
                pl.BlockSpec((sources, top_count, tokens), lambda n, e: (0, 0, 0)),
                pl.BlockSpec((sources, capacity, hidden_units), lambda n, e: (0, 0, 0)),
                pl.BlockSpec((rows, step), lambda n, e: (0, n)),
            ],
            out_specs=pl.BlockSpec((hidden_units, step), lambda n, e: (0, n)),
            scratch_shapes=[pltpu.VMEM((hidden_units, rows), BF16)],
        ),
        compiler_params=pltpu.CompilerParams(vmem_limit_bytes=VMEM_LIMIT),
        name="weight_sum",
    )(scalars, ids_all, recv_hidden, grads)


RING = 8
COLUMNS = 4
COPIES = 2 * COLUMNS + 1
ADD_LIMIT = 24 * 1024 * 1024
ID_ROWS = 8
PARTS = 4
UNPACK_FLOPS = 40_000_000_000
OFFSETS = (0, -1, 1, -2, 2, -3, 3, 4)
SWAP = [(i, i ^ 1) for i in range(16)]


def ring_device(position, core):
    z, y = (position, 0) if position < 4 else (7 - position, 1)
    return (z * 2 + y) * 2 + core


def ring_shift(step):
    return [
        (ring_device(p, core), ring_device((p + step) % RING, core))
        for p in range(RING)
        for core in range(2)
    ]


def ring_position(device):
    z, y = device >> 2, (device >> 1) & 1
    return jnp.where(y == 0, z, 7 - z)


def ring_pack_kernel(capacity, me_ref, ids_ref, gates_ref, hidden_ref, *rest):
    outs, (place_ref, table, select, blocks, sems) = rest[:RING], rest[RING:]
    top_count, tokens = ids_ref.shape
    experts = 2 * RING
    expert = lax.broadcasted_iota(I32, (experts, tokens), 0)
    named = jnp.zeros((experts, tokens), F32)
    for k in range(top_count):
        named = named + (ids_ref[k : k + 1, :] == expert).astype(F32)
    rank = jnp.dot(named.astype(BF16), earlier(tokens), preferred_element_type=F32).astype(I32)
    me = me_ref[0]
    target = (ring_position(expert) * 2 + ((expert & 1) ^ (me & 1))) * capacity + rank
    for k in range(top_count):
        place_ref[k : k + 1, :] = jnp.sum(
            jnp.where(ids_ref[k : k + 1, :] == expert, target, 0), axis=0, keepdims=True
        )
        table[k * tokens : (k + 1) * tokens, :] = hidden_ref[k]
    step = 2 * capacity
    copies = []
    for d in range(RING):
        row = lax.broadcasted_iota(I32, (step, tokens), 0) + ((ring_position(me) + d) & 7) * step
        for k in range(top_count):
            select[:, k * tokens : (k + 1) * tokens] = jnp.where(
                place_ref[k : k + 1, :] == row, gates_ref[k : k + 1, :].astype(F32), 0.0
            ).astype(BF16)
        blocks[d] = jnp.dot(select[...], table[...], preferred_element_type=F32).astype(BF16)
        copies.append(pltpu.make_async_copy(blocks.at[d], outs[d], sems.at[d]))
        copies[-1].start()
    for copy in copies:
        copy.wait()


def ring_pack(me, ids_t, gates_t, hidden_t, capacity):
    top_count, tokens, hidden_units = hidden_t.shape
    block = jax.ShapeDtypeStruct((2 * capacity, hidden_units), BF16)
    *blocks, place = pl.pallas_call(
        functools.partial(ring_pack_kernel, capacity),
        out_shape=(block,) * RING + (jax.ShapeDtypeStruct((top_count, tokens), I32),),
        in_specs=[whole(pltpu.SMEM)] + [whole()] * 3,
        out_specs=(whole(pltpu.HBM),) * RING + (whole(),),
        scratch_shapes=[
            pltpu.VMEM((top_count * tokens, hidden_units), BF16),
            pltpu.VMEM((2 * capacity, top_count * tokens), BF16),
            pltpu.VMEM((RING, 2 * capacity, hidden_units), BF16),
            pltpu.SemaphoreType.DMA((RING,)),
        ],
        compiler_params=pltpu.CompilerParams(vmem_limit_bytes=VMEM_LIMIT),
        cost_estimate=pl.CostEstimate(flops=3_000_000_000, bytes_accessed=5_000_000, transcendentals=0),
        name="pack",
    )(me, ids_t, gates_t, hidden_t)
    return blocks, place


def both_ranks(ids, me, capacity, tokens):
    own = source_rank(ids, me, tokens)
    other = source_rank(ids, me ^ 1, tokens)
    return own, jnp.where(other >= 0, other + capacity, -1)


def load(refs, buffer, sems, first):
    copies, at = [], 0
    for n, ref in enumerate(refs):
        copies.append(
            pltpu.make_async_copy(ref, buffer.at[pl.ds(at, ref.shape[0])], sems.at[first + n])
        )
        copies[-1].start()
        at += ref.shape[0]
    return copies


def load_pieces(refs, grads, ids, sems, first):
    half, wide = ids.shape[2] // 2, grads.shape[1] // COLUMNS
    rows, routes, at = [], [], 0
    for ref in refs:
        extra = ref.shape[0] % 16
        for base in range(0, ref.shape[0] - extra, half * COLUMNS):
            for column in range(COLUMNS):
                rows.append(
                    pltpu.make_async_copy(
                        ref.at[pl.ds(base + column * half, half)],
                        grads.at[pl.ds(at, half), pl.ds(column * wide, wide)],
                        sems.at[first + len(rows) + len(routes)],
                    )
                )
            at += half
        if extra:
            routes.append(
                pltpu.make_async_copy(
                    ref.at[pl.ds(ref.shape[0] - extra, extra), pl.ds(0, 2 * half)],
                    ids.at[at // (2 * half) - 1],
                    sems.at[first + len(rows) + len(routes)],
                )
            )
    for copy in routes + rows:
        copy.start()
    return routes, rows


def ring_upstream_kernel(capacity, offsets, pieces, me_ref, own_ref, other_ref, *rest):
    blocks = len(offsets)
    grad_refs, (out_ref, weights, grads, ids, dense, rows, sems, out_sems) = rest[:pieces], rest[-8:]
    tokens = ids.shape[2]
    me = me_ref[0]
    routes, loads = load_pieces(grad_refs, grads, ids, sems, 2)
    loads += routes
    weight_loads = [
        pltpu.make_async_copy(own_ref, weights.at[0], sems.at[0]),
        pltpu.make_async_copy(other_ref, weights.at[1], sems.at[1]),
    ]
    for copy in weight_loads:
        copy.start()
    for copy in loads:
        copy.wait()
    for i in range(2):
        weight_loads[i].wait()
        product = lax.dot_general(
            grads[...], weights[i], (((1,), (1,)), ((), ())), preferred_element_type=F32
        ).astype(BF16)
        for b in range(blocks):
            dense[b, i * tokens : (i + 1) * tokens, :] = product[b * tokens : (b + 1) * tokens, :]
    row = lax.broadcasted_iota(I32, (2 * capacity, 2 * tokens), 0)
    copies = []
    for b, offset in enumerate(offsets):
        ranks = both_ranks(ids[b].astype(F32).astype(I32), me, capacity, tokens)
        choose = (jnp.concatenate(ranks, axis=1) == row).astype(F32).astype(BF16)
        rows[b] = jnp.dot(choose, dense[b], preferred_element_type=F32).astype(BF16)
        goal = out_ref.at[(ring_position(me) + offset + RING) & 7]
        copies.append(pltpu.make_async_copy(rows.at[b], goal, out_sems.at[b]))
        copies[-1].start()
    for copy in copies:
        copy.wait()


def ring_upstream(me, tokens, offsets, pieces, so_far, own_weight, other_weight, capacity):
    hidden_units, width = own_weight.shape
    blocks = len(offsets)
    return pl.pallas_call(
        functools.partial(ring_upstream_kernel, capacity, offsets, len(pieces)),
        out_shape=jax.ShapeDtypeStruct((RING, 2 * capacity, hidden_units), BF16),
        in_specs=[whole(pltpu.SMEM)] + [whole(pltpu.HBM)] * (2 + len(pieces) + len(so_far)),
        out_specs=whole(pltpu.HBM),
        input_output_aliases={3 + len(pieces): 0} if so_far else {},
        scratch_shapes=[
            pltpu.VMEM((2, hidden_units, width), BF16),
            pltpu.VMEM((blocks * tokens, width), BF16),
            pltpu.VMEM((blocks, ID_ROWS, tokens), BF16),
            pltpu.VMEM((blocks, 2 * tokens, hidden_units), BF16),
            pltpu.VMEM((blocks, 2 * capacity, hidden_units), BF16),
            pltpu.SemaphoreType.DMA((2 + COPIES * blocks,)),
            pltpu.SemaphoreType.DMA((blocks,)),
        ],
        compiler_params=pltpu.CompilerParams(vmem_limit_bytes=VMEM_LIMIT),
        cost_estimate=pl.CostEstimate(
            flops=4 * blocks * tokens * hidden_units * width,
            bytes_accessed=2 * (blocks * tokens + 2 * hidden_units) * width,
            transcendentals=0,
        ),
        name="upstream",
    )(me, own_weight, other_weight, *pieces, *so_far)


def ring_weight_kernel(capacity, other, pieces, me_ref, *rest):
    grad_refs, hidden_refs = rest[:pieces], rest[pieces : pieces + RING]
    outs, (grads, ids, hidden, dense, sems) = rest[pieces + RING : -5], rest[-5:]
    tokens = ids.shape[2]
    me = me_ref[0]
    routes, grad_loads = load_pieces(grad_refs, grads, ids, sems, 0)
    loads = [
        pltpu.make_async_copy(ref, hidden.at[q], sems.at[COPIES * RING + q])
        for q, ref in enumerate(hidden_refs)
    ]
    for copy in loads:
        copy.start()
    for copy in routes + loads:
        copy.wait()
    row = lax.broadcasted_iota(I32, (2 * capacity, tokens), 0)
    for q in range(RING):
        rank = both_ranks(ids[q].astype(F32).astype(I32), me, capacity, tokens)[other]
        choose = (rank == row).astype(F32).astype(BF16)
        dense[:, q * tokens : (q + 1) * tokens] = lax.dot_general(
            hidden[q], choose, (((0,), (0,)), ((), ())), preferred_element_type=F32
        ).astype(BF16)
    for copy in grad_loads:
        copy.wait()
    width = grads.shape[1]
    step = 1280

    @pl.loop(0, width // step)
    def _(n):
        at = pl.ds(pl.multiple_of(n * step, step), step)
        total = jnp.dot(dense[...], grads[:, at], preferred_element_type=F32)
        height = total.shape[0] // len(outs)
        for part, part_ref in enumerate(outs):
            part_ref[:, at] = total[part * height : (part + 1) * height].astype(BF16)


def ring_weight_sum(me, tokens, pieces, hidden, other, capacity):
    width = pieces[0].shape[1] * COLUMNS
    hidden_units = hidden[0].shape[1]
    result = jax.ShapeDtypeStruct((hidden_units // PARTS, width), BF16)
    return pl.pallas_call(
        functools.partial(ring_weight_kernel, capacity, other, len(pieces)),
        out_shape=(result,) * PARTS,
        in_specs=[whole(pltpu.SMEM)] + [whole(pltpu.HBM)] * (len(pieces) + RING),
        out_specs=(whole(),) * PARTS,
        scratch_shapes=[
            pltpu.VMEM((RING * tokens, width), BF16),
            pltpu.VMEM((RING, ID_ROWS, tokens), BF16),
            pltpu.VMEM((RING, 2 * capacity, hidden_units), BF16),
            pltpu.VMEM((hidden_units, RING * tokens), BF16),
            pltpu.SemaphoreType.DMA((COPIES * RING + RING,)),
        ],
        compiler_params=pltpu.CompilerParams(vmem_limit_bytes=VMEM_LIMIT),
        cost_estimate=pl.CostEstimate(flops=1_000_000, bytes_accessed=1_000_000, transcendentals=0),
        name="weight_other" if other else "weight_own",
    )(me, *pieces, *hidden)


def add_kernel(trained_ref, *rest):
    own_refs, came_refs, (out_ref, own, came, sums, sems) = rest[:PARTS], rest[PARTS : 2 * PARTS], rest[-5:]
    trained = trained_ref[0].astype(F32)
    height = own.shape[1]
    loads = []
    for part in range(PARTS):
        for n, (ref, buffer) in enumerate(((own_refs[part], own), (came_refs[part], came))):
            loads.append(pltpu.make_async_copy(ref, buffer.at[part], sems.at[n, part]))
            loads[-1].start()
    stores = []
    for part in range(PARTS):
        loads[2 * part].wait()
        loads[2 * part + 1].wait()
        total = own[part].astype(F32) + came[part].astype(F32)
        sums[part] = (total * trained).astype(BF16)
        goal = out_ref.at[pl.ds(part * height, height)]
        stores.append(pltpu.make_async_copy(sums.at[part], goal, sems.at[2, part]))
        stores[-1].start()
    for copy in stores:
        copy.wait()


def add_parts(trained, own, came):
    height, width = own[0].shape
    return pl.pallas_call(
        add_kernel,
        out_shape=jax.ShapeDtypeStruct((height * PARTS, width), BF16),
        in_specs=[whole(pltpu.SMEM)] + [whole(pltpu.HBM)] * (2 * PARTS),
        out_specs=whole(pltpu.HBM),
        scratch_shapes=[pltpu.VMEM((PARTS, height, width), BF16)] * 3
        + [pltpu.SemaphoreType.DMA((3, PARTS))],
        compiler_params=pltpu.CompilerParams(vmem_limit_bytes=ADD_LIMIT),
        cost_estimate=pl.CostEstimate(flops=1_000_000, bytes_accessed=1_000_000, transcendentals=0),
        name="weight_add",
    )(trained, *own, *came)


def unpack_kernel(place_ref, gates_ref, hidden_ref, back_ref, grad_ref, gate_ref, select, sums):
    tokens, top_count = place_ref.shape
    rows = back_ref.shape[0]
    lane = lax.broadcasted_iota(I32, (tokens, rows), 1)
    for k in range(top_count):
        select[k * tokens : (k + 1) * tokens, :] = (
            (place_ref[:, k : k + 1] == lane).astype(F32).astype(BF16)
        )
    sums[...] = jnp.zeros_like(sums)
    step = 256
    totals = [0.0] * top_count
    for first in range(0, back_ref.shape[1], step):
        units = slice(first, first + step)
        up = jnp.dot(select[...], back_ref[:, units], preferred_element_type=F32)
        for k in range(top_count):
            mine = up[k * tokens : (k + 1) * tokens, :]
            grad_ref[k, :, units] = (gates_ref[:, k : k + 1].astype(F32) * mine).astype(BF16)
            products = hidden_ref[k, :, units].astype(F32) * mine
            totals[k] = totals[k] + jnp.sum(products, axis=1, keepdims=True)
    for k in range(top_count):
        sums[:, k : k + 1] = totals[k]
    gate_ref[...] = sums[...].T[:top_count, :].astype(BF16)


def unpack(place, gates, hidden_t, back):
    top_count, tokens, hidden_units = hidden_t.shape
    rows = sum(block.shape[0] for block in back)
    return pl.pallas_call(
        unpack_kernel,
        out_shape=(
            jax.ShapeDtypeStruct((top_count, tokens, hidden_units), BF16),
            jax.ShapeDtypeStruct((top_count, tokens), BF16),
        ),
        in_specs=[whole()] * 3 + [whole()] * len(back),
        out_specs=(whole(), whole()),
        scratch_shapes=[
            pltpu.VMEM((top_count * tokens, rows), BF16),
            pltpu.VMEM((tokens, 128), F32),
        ],
        compiler_params=pltpu.CompilerParams(vmem_limit_bytes=16 * 1024 * 1024),
        cost_estimate=pl.CostEstimate(
            flops=UNPACK_FLOPS, bytes_accessed=6 * rows * hidden_units, transcendentals=0
        ),
        name="unpack",
    )(place, gates, hidden_t, *back)


def ring_exchange(out_grad, hidden_t, ids_t, gates_t, scalars, weight, capacity):
    def send(value, step):
        return lax.ppermute(value, "expert", ring_shift(step))

    me = scalars[:1]
    tokens, width = out_grad.shape
    half, wide = tokens // 2, width // COLUMNS
    cut = half * COLUMNS
    rows = out_grad.reshape(2, half, COLUMNS, wide).transpose(0, 2, 1, 3).reshape(2 * cut, wide)
    spare = ((0, ID_ROWS - ids_t.shape[0]), (0, wide - tokens))
    block = jnp.concatenate([rows, jnp.pad(ids_t.astype(BF16), spare, constant_values=-1)])
    packed, place = ring_pack(me, ids_t, gates_t, hidden_t, capacity)
    other_weight = lax.ppermute(weight, "expert", SWAP)
    barrier = lax.optimization_barrier
    hidden = [None] * RING

    def send_hidden(*chosen):
        for q in chosen:
            hidden[q] = send(packed[-OFFSETS[q] % RING], -OFFSETS[q] % RING)

    ahead, behind = send(block, 1), send(block, -1)
    ahead, behind, *packed = barrier((ahead, behind, *packed))
    pieces = [block, ahead, behind]
    hidden[0] = packed[0]
    ahead, behind = send(ahead, 1), send(behind, -1)
    ahead, behind, other_weight = barrier((ahead, behind, other_weight))
    pieces += [ahead, behind]
    upstream_of = functools.partial(
        ring_upstream, me, tokens, own_weight=weight, other_weight=other_weight, capacity=capacity
    )
    ahead, behind = send(ahead, 1), send(behind, -1)
    send_hidden(1, 2)
    up = upstream_of(OFFSETS[:5], pieces[:5], ())
    pieces += [ahead, behind]
    ahead, behind, hidden[1], hidden[2], up = barrier(
        (ahead[:cut], behind[cut:], hidden[1], hidden[2], up)
    )
    pieces += [send(ahead, 1), send(behind, -1)]
    send_hidden(7, 5, 6, 3, 4)
    up = upstream_of(OFFSETS[5:], pieces[5:], (up,))
    *hidden, up = barrier((*hidden, up))
    groups = [[ring_device(p, core) for p in range(RING)] for core in range(2)]
    back = lax.all_to_all(up, "expert", 0, 0, axis_index_groups=groups, tiled=True)
    theirs = ring_weight_sum(me, tokens, pieces, hidden, True, capacity)
    came = [lax.ppermute(part, "expert", SWAP) for part in theirs]
    own = ring_weight_sum(me, tokens, pieces, hidden, False, capacity)
    weight_grad = add_parts(scalars[1:], own, came)
    place, weight_grad = barrier((place, weight_grad))
    return place, [back.reshape(-1, back.shape[2])], weight_grad


def gather_exchange(out_grad, hidden_t, ids_t, gates_t, scalars, weight, capacity):
    experts = lax.axis_size("expert")
    hidden_units = weight.shape[0]
    ids_all = lax.all_gather(ids_t, "expert", axis=0)
    packed, place = pack(ids_t, gates_t, hidden_t, experts, capacity)
    grads = lax.all_gather(out_grad, "expert", axis=0, tiled=True)
    recv_hidden = lax.all_to_all(
        packed.reshape(experts, capacity, hidden_units), "expert", 0, 0, tiled=True
    )
    up = upstream(scalars[:1], ids_all, grads, weight, capacity)
    back = lax.all_to_all(up, "expert", 0, 0, tiled=True)
    weight_grad = weight_sum(scalars, ids_all, recv_hidden, grads)
    return place, [back.reshape(experts * capacity, hidden_units)], weight_grad


def local(out_grad, saved_hidden, expert_ids, gate_weights, trained, down_weight):
    experts = lax.axis_size("expert")
    tokens, top_count, _ = saved_hidden.shape
    capacity = min(tokens, 3 * tokens * top_count // (2 * experts))
    hidden_t = saved_hidden.transpose(1, 0, 2)
    scalars = jnp.stack([lax.axis_index("expert").astype(I32), trained[0]])
    exchange = ring_exchange if experts == 2 * RING else gather_exchange
    place, back, weight_grad = exchange(
        out_grad, hidden_t, expert_ids.T, gate_weights.T, scalars, down_weight[0], capacity
    )
    hidden_grad, gate_grad = unpack(place.T, gate_weights, hidden_t, back)
    return hidden_grad.transpose(1, 0, 2), gate_grad.T, weight_grad[None]


def solution(mesh):
    placed = (
        P(("groups", "expert"), None),
        P(("groups", "expert"), None, None),
        P(("groups", "expert"), None),
        P(("groups", "expert"), None),
        P(("groups", "expert")),
        P("expert", None, None),
    )
    return jax.shard_map(
        local,
        mesh=mesh,
        in_specs=placed,
        out_specs=(
            P(("groups", "expert"), None, None),
            P(("groups", "expert"), None),
            P(("groups", "expert"), None, None),
        ),
        check_vma=False,
    )
```
